256 devices in a mesh: dp: 64 (over z, x, core), mp: 4 (over y).
Axes of the slice: x: 4, y: 4, z: 8, core: 2. Of those that a mesh axis runs over, the one named last changes fastest.
Arguments:
- features: bfloat16 [262144, 1024], P('dp'), may hold values from -6 to 6
- w_in: bfloat16 [1024, 1024], P(None, 'mp'), may hold values from -0.1875 to 0.1875
- w_out: bfloat16 [1024, 128], P('mp'), may hold values from -0.1875 to 0.1875
- send_rows: int32 [524288], P(('dp', 'mp')), may hold values from 0 to 1023
- pair_src: int32 [262144, 16], P(('dp', 'mp')), may hold values from 0 to 2047
- pair_weight: float32 [262144, 16], P(('dp', 'mp')), may hold values from 0.1 to 1
- pair_mask: int32 [262144, 16], P(('dp', 'mp')), may hold values 0 or 1
Outputs:
- grad_in: float32 [1024, 1024], P(None, 'mp')
- grad_out: float32 [1024, 128], P('mp')
The draws below stay inside these ranges and needn't reach their ends.
Inputs may be any that keep to these rules, and one draw needn't show every extreme that they name: `send_rows`: local row indices of the sending device.
All inputs are finite; a program needn't handle non-finite values. No bound on the sum of `pair_mask` on one device may be relied on, other than what follows from the above.
Results may differ from the reference program's by a relative error of at most 0.0062.
Values may be sent and summed in bfloat16 or wider, within the bound.
A program may use at most 128 MiB of HBM per device.

```python
import math
import jax
import jax.numpy as jnp
from jax import lax

DIN = 1024
H = 1024
K = 128
P_SIZE = 16
NODE_DEV = 4096
RECV_DEV = 2048
NODES = 262144
ROWS = 1024
SLOTS = 32
SENDS = 524288
N_DP = 64
N_MP = 4


def touch_ends(values, own_key, smallest, largest):
    longest = values.shape.index(max(values.shape))
    spots = []
    for shift in (0, 1):
        where = [jax.random.randint(jax.random.fold_in(own_key, axis), (), 0, length) for axis, length in enumerate(values.shape)]
        where[longest] = (where[longest] + shift) % values.shape[longest]
        spots.append(tuple(where))
    return values.at[spots[0]].set(smallest).at[spots[1]].set(largest)


def block_scale(key, shape, cuts, smallest, largest):
    factor_of, own = 1.0, jax.random.fold_in(key, 6)
    for position, parts in cuts:
        steps = jnp.exp(jax.random.uniform(jax.random.fold_in(own, position), (parts,), jnp.float32, smallest / len(cuts), largest / len(cuts)))
        factor_of = factor_of * jnp.repeat(steps, shape[position] // parts).reshape([-1 if axis == position else 1 for axis in range(len(shape))])
    return factor_of


def noise(rng, extent, deviation, bound, split=(), held_as=jnp.bfloat16):
    result = jax.random.normal(rng, extent, jnp.float32) * deviation
    if len(split) > 0:
        result = block_scale(rng, extent, split, -0.22, 0.18) * result
    return jnp.clip(result, min=-bound, max=bound).astype(held_as)


def setup_inputs(seed: int = 0) -> dict:
    splits = jax.random.split(jax.random.key(seed), 8)
    return {
        "features": noise(splits[0], (NODES, DIN), 1.0, 6.0, ((0, 64),)),
        "w_in": noise(splits[1], (DIN, H), DIN ** -0.5, 0.1875, ((1, 4),)),
        "w_out": noise(splits[2], (H, K), H ** -0.5, 0.1875, ((0, 4),)),
        "send_rows": touch_ends(jax.random.randint(splits[3], (SENDS,), 0, ROWS), jax.random.fold_in(splits[3], 1), 0, ROWS - 1).astype(jnp.int32),
        "pair_src": touch_ends(jax.random.randint(splits[4], (NODES, P_SIZE), 0, RECV_DEV), jax.random.fold_in(splits[4], 1), 0, RECV_DEV - 1).astype(jnp.int32),
        "pair_weight": jnp.clip(jnp.exp(math.log(1.0) - 2.3025851 * jax.random.uniform(splits[5], (NODES, P_SIZE), jnp.float32) ** block_scale(splits[5], (NODES, P_SIZE), ((0, 256),), -0.2, 0.2)), 0.1, 1.0),
        "pair_mask": touch_ends((jax.random.randint(splits[6], (NODES, P_SIZE), 0, 4) < 3).astype(jnp.int32), jax.random.fold_in(splits[6], 1), 0, 1),
    }


def reference(features, w_in, w_out, send_rows, pair_src, pair_weight, pair_mask):
    high = lax.Precision.HIGHEST
    blocks = features.reshape(N_DP, NODE_DEV, DIN)

    def forward(block):
        hidden = jax.nn.silu(jnp.dot(block.astype(jnp.float32), w_in.astype(jnp.float32), preferred_element_type=jnp.float32)).astype(jnp.bfloat16)
        return jnp.dot(hidden.astype(jnp.float32), w_out.astype(jnp.float32), preferred_element_type=jnp.float32)
    embed = lax.map(forward, blocks).reshape(NODES, K)
    gram = jnp.dot(embed.T, embed, precision=high) / NODES
    chol = jnp.linalg.cholesky(gram)
    white = lax.linalg.triangular_solve(chol, embed, left_side=False, lower=True, transpose_a=True)
    shards = N_DP * N_MP
    dev = jnp.arange(shards, dtype=jnp.int32)[:, None]
    slot = jnp.arange(RECV_DEV, dtype=jnp.int32)[None, :]
    source = slot // SLOTS * N_MP + dev % N_MP
    local_idx = send_rows[source * RECV_DEV + dev // N_MP * SLOTS + slot % SLOTS]
    table = (source * ROWS + local_idx).astype(jnp.int32)
    scale = 1.0 / (P_SIZE * math.sqrt(NODES))
    coef = pair_weight * pair_mask.astype(jnp.float32) * scale

    def visit(acc, item):
        rows_z, src, cs, tab = item
        partner = tab[src]
        diff = rows_z[:, None, :] - white[partner]
        own = 2.0 * lax.optimization_barrier(jnp.sum(cs[:, :, None] * diff, axis=1))
        acc = acc.at[partner.reshape(-1)].add((-2.0 * cs[:, :, None] * diff).reshape(-1, K))
        return (acc, own)
    init = jnp.zeros((NODES, K), jnp.float32)
    acc, owns = lax.scan(visit, init, (white.reshape(shards, ROWS, K), pair_src.reshape(shards, ROWS, P_SIZE), coef.reshape(shards, ROWS, P_SIZE), table))
    grad_z = owns.reshape(NODES, K) + acc
    curv = jnp.dot(white.T, grad_z, precision=high)
    inner = grad_z - jnp.dot(white, curv, precision=high) / NODES
    grad_y = lax.linalg.triangular_solve(chol, inner, left_side=False, lower=True, transpose_a=False).astype(jnp.bfloat16)

    def backward(carry, item):
        block, gy = item
        pre = jnp.dot(block.astype(jnp.float32), w_in.astype(jnp.float32), preferred_element_type=jnp.float32)
        hidden = jax.nn.silu(pre).astype(jnp.bfloat16)
        g_out = carry[1] + jnp.dot(hidden.T.astype(jnp.float32), gy.astype(jnp.float32), preferred_element_type=jnp.float32)
        dh = jnp.dot(gy.astype(jnp.float32), w_out.T.astype(jnp.float32), preferred_element_type=jnp.float32)
        sig = jax.nn.sigmoid(pre)
        grad_pre = (dh * sig * (1.0 + pre * (1.0 - sig))).astype(jnp.bfloat16)
        g_in = carry[0] + jnp.dot(block.T.astype(jnp.float32), grad_pre.astype(jnp.float32), preferred_element_type=jnp.float32)
        return ((g_in, g_out), None)
    start = (jnp.zeros((DIN, H), jnp.float32), jnp.zeros((H, K), jnp.float32))
    (grad_in, grad_out), _ = lax.scan(backward, start, (blocks, grad_y.reshape(N_DP, NODE_DEV, K)))
    return (grad_in, grad_out)
```

```python
import functools
import math

import jax
import jax.numpy as jnp
from jax import lax
from jax.experimental import pallas as pl
from jax.experimental.pallas import tpu as pltpu
from jax.sharding import PartitionSpec as P

MESH = pl.DeviceIdType.MESH
HIGH = lax.Precision.HIGHEST
F32 = jnp.float32
BF16 = jnp.bfloat16
NX = 4
NC = 2


def dot(a, b, dims=((1,), (0,)), precision=None):
    return lax.dot_general(a, b, (dims, ((), ())), precision=precision, preferred_element_type=F32)


def split(v):
    hi = v.astype(BF16)
    return hi, (v - hi.astype(F32)).astype(BF16)


def remote(src, dst, ssem, rsem, where):
    return pltpu.make_async_remote_copy(
        src_ref=src, dst_ref=dst, send_sem=ssem, recv_sem=rsem, device_id=where, device_id_type=MESH
    )


def drain(view, sem):
    pltpu.make_async_copy(view, view, sem).wait()


def kernel(
    n_dp, n_mp, nodes, factor,
    x_hbm, w_in, w_out, src, weight, mask, rows_of, all_i, all_o,
    xv, hv, dv, ypv, ot, at, s16, cw, abuf, bsend, bbuf, ybf, sbuf, rbuf, tbuf, qbuf, aty, degs, own, hib, lob,
    d_send, d_in, d_all, pc, gacc, oacc, gi, go,
    g_send, g_in, g_x, g_y, g_all, w,
    ci_r, co_r, xi_s, xo_s, xi_r, xo_r, zi_s, zo_s, zi_r, zo_r,
    ld_s, rs_s, rs_r, x_s, x_r, ar_s, ar_r, ag_s, ag_r, s_s, s_r, b_s, b_r,
):
    me = lax.axis_index("dp")
    my = lax.axis_index("mp")
    nz = n_dp // (NX * NC)
    ng = nz * NC
    zi, xi, ci = me // (NX * NC), me // NC % NX, me % NC
    gidx = zi * NC + ci
    right, left, opp = (my + 1) % n_mp, (my + n_mp - 1) % n_mp, (my + 2) % n_mp
    rows, width = ybf.shape
    half = rows // 2
    recv = rbuf.shape[0]
    slots = recv // n_dp
    pairs = src.shape[0]

    def load(i, q):
        some = pl.ds(pl.multiple_of(q * rows, rows), rows)
        return pltpu.make_async_copy(x_hbm.at[some], xv.at[some], ld_s.at[i])

    loads = [load(i, q) for i, q in enumerate((opp, right, left, my))]
    for c in loads:
        c.start()

    barrier = pltpu.get_barrier_semaphore()

    @pl.loop(1, n_dp)
    def _(k):
        pl.semaphore_signal(barrier, inc=1, device_id=((me + k) % n_dp, my), device_id_type=MESH)

    @pl.loop(1, n_mp)
    def _(k):
        pl.semaphore_signal(barrier, inc=1, device_id=(me, (my + k) % n_mp), device_id_type=MESH)

    def part_of(ref, q, part):
        return ref.at[pl.ds(pl.multiple_of(q * rows + part * half, half), half)]

    r_a = remote(part_of(ypv, opp, 0), abuf.at[0], rs_s.at[0], rs_r.at[0], (me, right))
    l_a = remote(part_of(ypv, opp, 1), abuf.at[1], rs_s.at[1], rs_r.at[1], (me, left))
    r_b = remote(bsend.at[0], bbuf.at[0, 1], rs_s.at[2], rs_r.at[2], (me, right))
    l_b = remote(bsend.at[1], bbuf.at[1, 0], rs_s.at[3], rs_r.at[3], (me, left))
    r_c = remote(bsend.at[2], bbuf.at[0, 0], rs_s.at[4], rs_r.at[4], (me, right))
    l_c = remote(bsend.at[3], bbuf.at[1, 1], rs_s.at[5], rs_r.at[5], (me, left))

    def pick(k, values):
        v = values[0]
        for i in range(1, len(values)):
            v = jnp.where(k == i, values[i], v)
        return v

    def forward(k, _):
        for i, at_step in enumerate((0, 2, 3, 6)):
            @pl.when(k == at_step)
            def _():
                loads[i].wait()

        q = pick(k, (opp, opp, right, left, right, left, my, my))
        part = pick(k, (0, 1, 1, 0, 0, 1, 0, 1))
        some = pl.ds(pl.multiple_of(q * rows + part * half, half), half)
        pre = dot(xv[some], w_in[...])
        sig = jax.nn.sigmoid(pre)
        hidden = (pre * sig).astype(BF16)
        hv[some] = hidden
        dv[some] = sig * (1.0 + pre * (1.0 - sig))
        ypv[some] = dot(hidden, w_out[...])

        @pl.when(k == 1)
        def _():
            def sel_body(g, _):
                base = pl.multiple_of(g * 32, 32)
                r = lax.broadcasted_iota(jnp.int32, (32, 128), 0) + base
                for lc in range(recv // 128):
                    lanes = slice(lc * 128, lc * 128 + 128)
                    hit = jnp.broadcast_to(rows_of[0:1, lanes], (32, 128)) == r
                    ot[pl.ds(base, 32), lanes] = jnp.where(hit, 1.0, 0.0).astype(BF16)
                return 0

            lax.fori_loop(0, rows // 32, sel_body, 0)

        @pl.when(k == 2)
        def _():
            pl.semaphore_wait(barrier, n_dp - 1 + n_mp - 1)
            r_a.start()
            l_a.start()
            bsend[0] = part_of(ypv, right, 1)[...].astype(BF16)
            r_b.start()

        @pl.when(k == 3)
        def _():
            bsend[1] = part_of(ypv, left, 0)[...].astype(BF16)
            l_b.start()

        return 0

    lax.fori_loop(0, 8, forward, 0)

    s_all, c_all = src[...], weight[...] * mask[...].astype(F32)
    total = c_all
    for k in range(1, pairs):
        hit = pltpu.roll(s_all, k, 0) == s_all
        total = total + jnp.where(hit, pltpu.roll(c_all, k, 0), 0.0)
    cw[...] = total.astype(BF16)
    s16[...] = s_all.astype(jnp.int16)

    span = 64

    def pair_chunk(lc):
        lanes = slice(lc * 128, lc * 128 + 128)
        s_l, c_l = s16[:, lanes], cw[:, lanes]
        ss = [jnp.broadcast_to(s_l[p : p + 1], (span, 128)) for p in range(pairs)]
        cs = [jnp.broadcast_to(c_l[p : p + 1], (span, 128)) for p in range(pairs)]

        def body(g, _):
            base = pl.multiple_of(g * span, span)
            r = (lax.broadcasted_iota(jnp.int32, (span, 128), 0) + base).astype(jnp.int16)
            acc = jnp.zeros((span, 128), BF16)
            for p in range(pairs):
                acc = jnp.where(ss[p] == r, cs[p], acc)
            at[pl.ds(base, span), lanes] = acc
            return 0

        lax.fori_loop(0, recv // span, body, 0)

    chunks = rows // 128
    for lc in range(chunks // 2):
        pair_chunk(lc)
    r_a.wait_recv()
    bsend[2] = (abuf[0] + part_of(ypv, right, 0)[...]).astype(BF16)
    r_c.start()
    l_a.wait_recv()
    bsend[3] = (abuf[1] + part_of(ypv, left, 1)[...]).astype(BF16)
    l_c.start()
    for lc in range(chunks // 2, chunks):
        pair_chunk(lc)
    for c in (r_b, l_b, r_c, l_c):
        c.wait_recv()
    y = (
        ypv[pl.ds(pl.multiple_of(my * rows, rows), rows)]
        + bbuf[0].reshape(rows, width).astype(F32)
        + bbuf[1].reshape(rows, width).astype(F32)
    )
    ybf[...] = y.astype(BF16)
    y_b = ybf[...]
    y_t = jnp.transpose(y_b.astype(F32)).astype(BF16)
    gram = dot(y_t, y_b)

    def group_device(k):
        return (k // NC * NX + xi) * NC + k % NC

    def sum_start(which, value):
        g_send[which] = value.reshape(ng, 8, width)
        g_in[which, gidx] = g_send[which, gidx]

        @pl.loop(1, ng)
        def _(k):
            peer = (gidx + k) % ng
            remote(g_send.at[which, peer], g_in.at[which, gidx], ar_s.at[which, 0], ar_r.at[which, 0], (group_device(peer), my)).start()

    def sum_x(which):
        drain(g_in.at[which, pl.ds(0, ng - 1)], ar_r.at[which, 0])
        t = g_in[which, 0]
        for k in range(1, ng):
            t = t + g_in[which, k]
        g_x[which, xi] = t
        for k in range(1, NX):
            peer = (zi * NX + (xi + k) % NX) * NC + ci
            remote(g_x.at[which, xi], g_x.at[which, xi], ar_s.at[which, 1], ar_r.at[which, 1], (peer, my)).start()

    def sum_y(which):
        drain(g_x.at[which, pl.ds(0, NX - 1)], ar_r.at[which, 1])
        t = g_x[which, 0]
        for k in range(1, NX):
            t = t + g_x[which, k]
        g_y[which, my] = t
        for k in range(1, n_mp):
            remote(g_y.at[which, my], g_y.at[which, my], ar_s.at[which, 2], ar_r.at[which, 2], (me, (my + k) % n_mp)).start()

    def sum_back(which):
        drain(g_y.at[which, pl.ds(0, n_mp - 1)], ar_r.at[which, 2])
        t = g_y[which, 0]
        for k in range(1, n_mp):
            t = t + g_y[which, k]
        g_all[which, gidx] = t

        @pl.loop(1, ng)
        def _(k):
            peer = (gidx + k) % ng
            remote(g_all.at[which, gidx], g_all.at[which, gidx], ar_s.at[which, 3], ar_r.at[which, 3], (group_device(peer), my)).start()

    def sum_end(which):
        drain(g_all.at[which, pl.ds(0, ng - 1)], ar_r.at[which, 3])
        return g_all[which].reshape(width, width) * (1.0 / nodes)

    sum_start(0, gram)

    def far_first(k):
        step = k + n_dp // 2
        return (me + step + step // n_dp) % n_dp

    def exchange(source, target, i):
        @pl.loop(0, n_dp - 1)
        def _(k):
            peer = far_first(k)
            remote(
                source.at[pl.ds(pl.multiple_of(peer * slots, slots), slots)],
                target.at[pl.ds(pl.multiple_of(me * slots, slots), slots)],
                x_s.at[i], x_r.at[i], (peer, my),
            ).start()

        mine = pl.ds(pl.multiple_of(me * slots, slots), slots)
        target[mine] = source[mine]

    def gather_body(k, _):
        lanes = pl.ds(pl.multiple_of(k * 256, 256), 256)
        sbuf[lanes] = jnp.transpose(dot(y_t, ot[:, lanes])).astype(BF16)
        return 0

    lax.fori_loop(0, recv // 256, gather_body, 0)
    exchange(sbuf, rbuf, 0)

    y_ones = jnp.concatenate([y_b, jnp.ones((rows, width), BF16)], axis=1)

    def aty_body(k, _):
        some = pl.ds(pl.multiple_of(k * 256, 256), 256)
        both = dot(at[some], y_ones)
        aty[some] = both
        whole = both[:, width:].astype(BF16).astype(F32)
        for j in range(2):
            d_send[2 * k + j] = jnp.transpose(whole[j * 128 : j * 128 + 128])[0:1]
        return 0

    lax.fori_loop(0, recv // 256, aty_body, 0)
    per = 128 // slots

    @pl.loop(0, n_dp - 1)
    def _(k):
        peer = far_first(k)
        remote(d_send.at[peer // per], d_in.at[me], x_s.at[2], x_r.at[2], (peer, my)).start()

    d_in[me] = d_send[me // per]
    ones_r = jnp.ones((width, recv), BF16)

    def deg_body(k, _):
        lanes = pl.ds(pl.multiple_of(k * 256, 256), 256)
        degs[lanes] = jnp.transpose(dot(ones_r, at[:, lanes]))
        return 0

    lax.fori_loop(0, rows // 256, deg_body, 0)
    sum_x(0)
    sum_y(0)
    sum_back(0)

    drain(rbuf.at[pl.ds(0, recv - slots)], x_r.at[0])
    r_t = jnp.transpose(rbuf[...].astype(F32)).astype(BF16)

    def back_body(k, _):
        some = pl.ds(pl.multiple_of(k * 256, 256), 256)
        both = aty[some]
        cross, d_all_k = both[:, :width], both[:, width:]
        r_k = rbuf[some].astype(F32)
        back = d_all_k * r_k - cross
        hi, lo = split(back)
        hib[some] = hi
        lob[some] = lo
        d_k = d_all_k.astype(BF16).astype(F32)
        tbuf[some] = (cross - (d_all_k - d_k) * r_k).astype(BF16)
        return 0

    lax.fori_loop(0, recv // 256, back_body, 0)

    def own_body(k, _):
        lanes = pl.ds(pl.multiple_of(k * 256, 256), 256)
        cross = jnp.transpose(dot(r_t, at[:, lanes]))
        own[lanes] = degs[lanes] * ybf[lanes].astype(F32) - cross
        return 0

    lax.fori_loop(0, rows // 256, own_body, 0)
    o_hi, o_lo = split(own[...])
    s_part = dot(y_t, o_hi) + dot(y_t, o_lo) + dot(r_t, hib[...]) + dot(r_t, lob[...])
    sum_start(1, s_part)
    exchange(tbuf, qbuf, 1)

    gram_n = sum_end(0)
    w[...] = gram_n
    lane = lax.broadcasted_iota(jnp.int32, (width, width), 1)
    sub = lax.broadcasted_iota(jnp.int32, (width, width), 0)

    def sweep(k, _):
        a = w[...]
        row = w[pl.ds(k, 1), :]
        on_lane = lane == k
        on_sub = sub == k
        col = jnp.sum(jnp.where(on_lane, a, 0.0), axis=1, keepdims=True)
        pivot = jnp.sum(jnp.where(on_lane[0:1], row, 0.0), axis=1, keepdims=True)
        inv = 1.0 / pivot
        scaled = row * inv
        new = a - col * scaled
        new = jnp.where(on_lane, col * inv, new)
        new = jnp.where(on_sub, jnp.where(on_lane, -inv, scaled), new)
        w[...] = new
        return 0

    lax.fori_loop(0, width // 4, sweep, 0)
    sum_x(1)
    lax.fori_loop(width // 4, width // 2, sweep, 0)
    sum_y(1)
    drain(d_in.at[pl.ds(0, n_dp - 1)], x_r.at[2])
    d_all[...] = pltpu.roll(d_in[...].reshape(n_dp, 128), (128 - slots * (me % per)) % 128, 1)
    spot = lax.broadcasted_iota(jnp.int32, (recv // 128, 128), 1) // slots
    d_row = jnp.zeros((recv // 128, 128), F32)
    for j in range(per):
        piece = d_all[pl.ds(j, recv // 128, stride=per), :]
        d_row = jnp.where(spot == j, pltpu.roll(piece, slots * j, 1), d_row)
    d_row = jnp.broadcast_to(d_row.reshape(1, recv), (width, recv)).astype(BF16)

    def add_body(k, _):
        some = pl.ds(pl.multiple_of(k * 256, 256), 256)
        extra = jnp.transpose(dot(d_row, ot[some], ((1,), (1,))))
        own[some] = own[some] + extra * ybf[some].astype(F32)
        return 0

    lax.fori_loop(0, rows // 256, add_body, 0)
    sum_back(1)
    lax.fori_loop(width // 2, width, sweep, 0)
    inv0 = -w[...]
    eye2 = jnp.where(lane == sub, 2.0, 0.0)
    inverse = dot(inv0, eye2 - dot(gram_n, inv0, precision=HIGH), precision=HIGH)
    i_hi, i_lo = split(inverse * factor)
    i_both = jnp.concatenate([i_hi, i_lo], axis=1)
    s_n = sum_end(1)
    b0 = dot(inverse, s_n, precision=HIGH)
    b1 = b0 + dot(inverse, s_n - dot(gram_n, b0, precision=HIGH), precision=HIGH)
    b_hi = b1.astype(BF16)
    rest = b1 - b_hi.astype(F32)
    b_mid = rest.astype(BF16)
    b_lo = (rest - b_mid.astype(F32)).astype(BF16)
    b_low = jnp.concatenate([b_mid, b_lo], axis=1)

    def remove_body(k, _):
        some = pl.ds(pl.multiple_of(k * 256, 256), 256)
        yk = ybf[some]
        low = dot(yk, b_low)
        own[some] = own[some] - (dot(yk, b_hi) + (low[:, :width] + low[:, width:]))
        return 0

    lax.fori_loop(0, rows // 256, remove_body, 0)
    drain(qbuf.at[pl.ds(0, recv - slots)], x_r.at[1])

    def grad_body(k, _):
        some = pl.ds(pl.multiple_of(k * 256, 256), 256)
        n_hi, n_lo = split(own[some] - dot(ot[some], qbuf[...]))
        both = dot(n_hi, i_both)
        gy = both[:, :width] + (both[:, width:] + dot(n_lo, i_hi))
        pc[pl.ds(pl.multiple_of(my * rows + k * 256, 256), 256)] = gy.astype(BF16)
        return 0

    lax.fori_loop(0, rows // 256, grad_body, 0)

    gathers = []
    for i, (q, part, to) in enumerate(
        ((my, 0, right), (my, 1, left), (my, 1, right), (my, 0, left), (left, 0, right), (right, 1, left))
    ):
        gathers.append(remote(part_of(pc, q, part), part_of(pc, q, part), ag_s.at[i], ag_r.at[i], (me, to)))
    for c in gathers[:4]:
        c.start()
    gacc[...] = jnp.zeros_like(gacc)
    oacc[...] = jnp.zeros_like(oacc)

    def backward(k, _):
        for i, (at_step, then) in enumerate(((2, 4), (3, 5), (4, None), (5, None), (6, None), (7, None))):
            @pl.when(k == at_step)
            def _():
                gathers[i].wait_recv()
                if then is not None:
                    gathers[then].start()

        q = pick(k, (my, my, left, right, left, right, opp, opp))
        part = pick(k, (0, 1, 0, 1, 1, 0, 0, 1))
        some = pl.ds(pl.multiple_of(q * rows + part * half, half), half)
        gy = pc[some]
        dh = dot(gy, w_out[...], ((1,), (1,)))
        gp_t = jnp.transpose(dh * dv[some]).astype(BF16)
        gacc[...] += dot(gp_t, xv[some])
        oacc[...] += dot(jnp.transpose(gy.astype(F32)).astype(BF16), hv[some])
        return 0

    lax.fori_loop(0, 8, backward, 0)
    gi[...] = jnp.transpose(gacc[...])
    go[...] = jnp.transpose(oacc[...])

    x, z, c = xi, zi, ci

    def at_x(k):
        return ((z * NX + k) * NC + c, my)

    def at_z(k):
        return ((k * NX + x) * NC + c, my)

    mate = (me - c + (1 - c), my)
    hi, ho = xi_s.shape[0], xo_s.shape[0]
    qi, qo = hi // NX, ho // NX
    ti = qi // nz
    theirs_i = pl.ds(pl.multiple_of((1 - c) * hi, hi), hi)
    theirs_o = pl.ds(pl.multiple_of((1 - c) * ho, ho), ho)
    mine_i = pl.ds(pl.multiple_of(c * hi, hi), hi)
    mine_o = pl.ds(pl.multiple_of(c * ho, ho), ho)
    c_i = remote(gi.at[theirs_i], ci_r, s_s.at[0], s_r.at[0], mate)
    c_o = remote(go.at[theirs_o], co_r, s_s.at[1], s_r.at[1], mate)
    c_i.start()
    c_o.start()
    c_i.wait_recv()
    c_o.wait_recv()
    ci_r[...] = gi[mine_i] + ci_r[...]
    co_r[...] = go[mine_o] + co_r[...]
    xi_s[...] = ci_r[...].astype(BF16)
    xo_s[...] = co_r[...].astype(BF16)
    sent = [c_i, c_o]
    xs = []
    for k in (2, 1, 3):
        p = (x + k) % NX
        a = remote(xi_s.at[pl.ds(pl.multiple_of(p * qi, qi), qi)], xi_r.at[k - 1], s_s.at[2 * k], s_r.at[2 * k], at_x(p))
        b = remote(xo_s.at[pl.ds(pl.multiple_of(p * qo, qo), qo)], xo_r.at[k - 1], s_s.at[2 * k + 1], s_r.at[2 * k + 1], at_x(p))
        a.start()
        b.start()
        xs += [a, b]
    for d in xs:
        d.wait_recv()
    sent += xs
    t_i = ci_r[pl.ds(pl.multiple_of(x * qi, qi), qi)]
    t_o = co_r[pl.ds(pl.multiple_of(x * qo, qo), qo)]
    for k in range(NX - 1):
        t_i = t_i + xi_r[k].astype(F32)
        t_o = t_o + xo_r[k].astype(F32)
    zi_s[...] = t_i.astype(BF16)
    zo_s[...] = t_o.astype(BF16)
    zo_r[z] = zo_s[...]
    zi_r[z] = zi_s[pl.ds(pl.multiple_of(z * ti, ti), ti)]
    order = sorted(range(1, nz), key=lambda k: -min(k, nz - k))
    for k in order:
        p = (z + k) % nz
        remote(zi_s.at[pl.ds(pl.multiple_of(p * ti, ti), ti)], zi_r.at[z], b_s.at[0], b_r.at[0], at_z(p)).start()
        remote(zo_s, zo_r.at[z], b_s.at[1], b_r.at[1], at_z(p)).start()

    drain(zi_r.at[pl.ds(0, nz - 1)], b_r.at[0])
    f_i = zi_r[0].astype(F32)
    for k in range(1, nz):
        f_i = f_i + zi_r[k].astype(F32)
    block_i = pl.ds(pl.multiple_of(c * hi + x * qi + z * ti, ti), ti)
    all_i[block_i] = f_i.astype(BF16)
    for k in order:
        remote(all_i.at[block_i], all_i.at[block_i], b_s.at[2], b_r.at[2], at_z((z + k) % nz)).start()
    drain(zo_r.at[pl.ds(0, nz - 1)], b_r.at[1])
    f_o = zo_r[0].astype(F32)
    for k in range(1, nz):
        f_o = f_o + zo_r[k].astype(F32)
    quarter_o = pl.ds(pl.multiple_of(c * ho + x * qo, qo), qo)
    all_o[quarter_o] = f_o.astype(BF16)
    for k in (2, 1, 3):
        remote(all_o.at[quarter_o], all_o.at[quarter_o], b_s.at[3], b_r.at[3], at_x((x + k) % NX)).start()
    drain(zi_s.at[pl.ds(0, (nz - 1) * ti)], b_r.at[2])
    quarter_i = pl.ds(pl.multiple_of(c * hi + x * qi, qi), qi)
    for k in (2, 1, 3):
        remote(all_i.at[quarter_i], all_i.at[quarter_i], b_s.at[4], b_r.at[4], at_x((x + k) % NX)).start()
    drain(xo_s.at[pl.ds(0, (NX - 1) * qo)], b_r.at[3])
    d_o = remote(all_o.at[mine_o], all_o.at[mine_o], b_s.at[5], b_r.at[5], mate)
    d_o.start()
    drain(xi_s.at[pl.ds(0, (NX - 1) * qi)], b_r.at[4])
    d_i = remote(all_i.at[mine_i], all_i.at[mine_i], b_s.at[6], b_r.at[6], mate)
    d_i.start()
    for which in range(2):
        drain(g_send.at[which, pl.ds(0, ng - 1)], ar_s.at[which, 0])
        drain(g_x.at[which, pl.ds(0, NX - 1)], ar_s.at[which, 1])
        drain(g_y.at[which, pl.ds(0, n_mp - 1)], ar_s.at[which, 2])
        drain(g_all.at[which, pl.ds(0, ng - 1)], ar_s.at[which, 3])
    for d in gathers + [r_a, l_a, r_b, l_b, r_c, l_c]:
        d.wait_send()
    drain(sbuf.at[pl.ds(0, recv - slots)], x_s.at[0])
    drain(tbuf.at[pl.ds(0, recv - slots)], x_s.at[1])
    drain(d_in.at[pl.ds(0, n_dp - 1)], x_s.at[2])
    drain(zi_r.at[pl.ds(0, nz - 1)], b_s.at[0])
    drain(zo_r.at[pl.ds(0, nz - 1)], b_s.at[1])
    drain(zi_s.at[pl.ds(0, (nz - 1) * ti)], b_s.at[2])
    drain(xo_s.at[pl.ds(0, (NX - 1) * qo)], b_s.at[3])
    drain(xi_s.at[pl.ds(0, (NX - 1) * qi)], b_s.at[4])
    for d in sent + [d_o, d_i]:
        d.wait_send()
    d_o.wait_recv()
    d_i.wait_recv()


def whole(features, w_in, w_out, src_t, weight_t, mask_t, send_row, n_dp, n_mp, nodes, factor):
    group, depth = features.shape
    units, width = w_out.shape
    rows = group // n_mp
    recv = send_row.shape[1]
    pairs = src_t.shape[0]
    nz = n_dp // (NX * NC)
    ng = n_dp // NX
    hi, ho = depth // NC, units // NC
    qi, qo = hi // NX, ho // NX
    vm = pltpu.VMEM
    dma = pltpu.SemaphoreType.DMA
    return pl.pallas_call(
        functools.partial(kernel, n_dp, n_mp, nodes, factor),
        out_shape=(jax.ShapeDtypeStruct((depth, units), BF16), jax.ShapeDtypeStruct((units, width), BF16)),
        in_specs=[pl.BlockSpec(memory_space=pl.ANY)] + [pl.BlockSpec(memory_space=vm)] * 6,
        out_specs=[pl.BlockSpec(memory_space=vm)] * 2,
        scratch_shapes=[
            vm((group, depth), BF16), vm((group, units), BF16), vm((group, units), F32), vm((group, width), F32),
            vm((rows, recv), BF16), vm((recv, rows), BF16), vm((pairs, rows), jnp.int16), vm((pairs, rows), BF16),
            vm((2, rows // 2, width), F32), vm((4, rows // 2, width), BF16), vm((2, 2, rows // 2, width), BF16),
            vm((rows, width), BF16),
            vm((recv, width), BF16), vm((recv, width), BF16), vm((recv, width), BF16), vm((recv, width), BF16),
            vm((recv, 2 * width), F32), vm((rows, width), F32), vm((rows, width), F32),
            vm((recv, width), BF16), vm((recv, width), BF16),
            vm((recv // 128, 1, 128), F32), vm((n_dp, 1, 128), F32), vm((n_dp, 128), F32),
            vm((group, width), BF16), vm((units, depth), F32), vm((width, units), F32),
            vm((depth, units), F32), vm((units, width), F32),
            vm((2, ng, 8, width), F32), vm((2, ng, 8, width), F32), vm((2, NX, 8, width), F32),
            vm((2, n_mp, 8, width), F32), vm((2, ng, 8, width), F32), vm((width, width), F32),
            vm((hi, units), F32), vm((ho, width), F32), vm((hi, units), BF16), vm((ho, width), BF16),
            vm((NX - 1, qi, units), BF16), vm((NX - 1, qo, width), BF16),
            vm((qi, units), BF16), vm((qo, width), BF16), vm((nz, qi // nz, units), BF16), vm((nz, qo, width), BF16),
            dma((4,)), dma((6,)), dma((6,)), dma((3,)), dma((3,)), dma((2, 4)), dma((2, 4)), dma((6,)), dma((6,)),
            dma((8,)), dma((8,)), dma((7,)), dma((7,)),
        ],
        compiler_params=pltpu.CompilerParams(collective_id=0, has_side_effects=True, vmem_limit_bytes=58 << 20),
        name="step",
    )(features, w_in, w_out, src_t, weight_t, mask_t, send_row)


def widen_kernel(a, b, oa, ob):
    oa[...] = a[...].astype(F32)
    ob[...] = b[...].astype(F32)


def widen(a, b):
    vm = pl.BlockSpec(memory_space=pltpu.VMEM)
    return pl.pallas_call(
        widen_kernel,
        out_shape=(jax.ShapeDtypeStruct(a.shape, F32), jax.ShapeDtypeStruct(b.shape, F32)),
        in_specs=[vm] * 2,
        out_specs=[vm] * 2,
        name="widen",
    )(a, b)


def shards(features, w_in, w_out, send_rows, pair_src, pair_weight, pair_mask):
    n_dp = lax.axis_size("dp")
    n_mp = lax.axis_size("mp")
    nodes = features.shape[0] * n_dp
    pairs = pair_src.shape[1]
    scale = 1.0 / (pairs * math.sqrt(nodes))
    return widen(
        *whole(
            features, w_in, w_out, pair_src.T, pair_weight.T, pair_mask.T, send_rows.reshape(1, -1),
            n_dp, n_mp, nodes, 2.0 * scale,
        )
    )


def solution(mesh):
    return jax.shard_map(
        shards,
        mesh=mesh,
        in_specs=(
            P("dp", None),
            P(None, "mp"),
            P("mp", None),
            P(("dp", "mp")),
            P(("dp", "mp"), None),
            P(("dp", "mp"), None),
            P(("dp", "mp"), None),
        ),
        out_specs=(P(None, "mp"), P("mp", None)),
        check_vma=False,
    )
```

```python
import functools
import math

import jax
import jax.numpy as jnp
from jax import lax
from jax.experimental import pallas as pl
from jax.experimental.pallas import tpu as pltpu
from jax.sharding import PartitionSpec as P

MESH = pl.DeviceIdType.MESH
HIGH = lax.Precision.HIGHEST
F32 = jnp.float32
BF16 = jnp.bfloat16
NX = 4
NC = 2


def dot(a, b, dims=((1,), (0,)), precision=None):
    return lax.dot_general(a, b, (dims, ((), ())), precision=precision, preferred_element_type=F32)


def split(v):
    hi = v.astype(BF16)
    return hi, (v - hi.astype(F32)).astype(BF16)


def remote(src, dst, ssem, rsem, where):
    return pltpu.make_async_remote_copy(
        src_ref=src, dst_ref=dst, send_sem=ssem, recv_sem=rsem, device_id=where, device_id_type=MESH
    )


def drain(view, sem):
    pltpu.make_async_copy(view, view, sem).wait()


def kernel(
    n_dp, n_mp, nodes, factor,
    x_hbm, w_in, w_out, src, weight, mask, rows_of, all_i, all_o,
    xv, hv, dv, ypv, ot, ot2, at, s16, cw, abuf, bsend, bbuf, ybf, sbuf, rbuf, tbuf, qbuf, aty, degs, own, hib, lob, qd,
    d_send, d_in, d_all, pc, gacc, oacc, gi, go,
    g_send, g_in, g_x, g_y, g_all, w,
    ci_r, co_r, xi_s, xo_s, xi_r, xo_r, zi_s, zo_s, zi_r, zo_r, zo_a,
    ld_s, rs_s, rs_r, x_s, x_r, ar_s, ar_r, ag_s, ag_r, s_s, s_r, b_s, b_r,
):
    me = lax.axis_index("dp")
    my = lax.axis_index("mp")
    nz = n_dp // (NX * NC)
    ng = nz * NC
    zi, xi, ci = me // (NX * NC), me // NC % NX, me % NC
    gidx = zi * NC + ci
    right, left, opp = (my + 1) % n_mp, (my + n_mp - 1) % n_mp, (my + 2) % n_mp
    rows, width = ybf.shape
    half = rows // 2
    recv = rbuf.shape[0]
    slots = recv // n_dp
    pairs = src.shape[0]

    def load(i, q):
        some = pl.ds(pl.multiple_of(q * rows, rows), rows)
        return pltpu.make_async_copy(x_hbm.at[some], xv.at[some], ld_s.at[i])

    loads = [load(i, q) for i, q in enumerate((opp, right, left, my))]
    for c in loads:
        c.start()

    barrier = pltpu.get_barrier_semaphore()

    @pl.loop(1, n_dp)
    def _(k):
        pl.semaphore_signal(barrier, inc=1, device_id=((me + k) % n_dp, my), device_id_type=MESH)

    @pl.loop(1, n_mp)
    def _(k):
        pl.semaphore_signal(barrier, inc=1, device_id=(me, (my + k) % n_mp), device_id_type=MESH)

    def part_of(ref, q, part):
        return ref.at[pl.ds(pl.multiple_of(q * rows + part * half, half), half)]

    r_a = remote(part_of(ypv, opp, 0), abuf.at[0], rs_s.at[0], rs_r.at[0], (me, right))
    l_a = remote(part_of(ypv, opp, 1), abuf.at[1], rs_s.at[1], rs_r.at[1], (me, left))
    r_b = remote(bsend.at[0], bbuf.at[0, 1], rs_s.at[2], rs_r.at[2], (me, right))
    l_b = remote(bsend.at[1], bbuf.at[1, 0], rs_s.at[3], rs_r.at[3], (me, left))
    r_c = remote(bsend.at[2], bbuf.at[0, 0], rs_s.at[4], rs_r.at[4], (me, right))
    l_c = remote(bsend.at[3], bbuf.at[1, 1], rs_s.at[5], rs_r.at[5], (me, left))

    def pick(k, values):
        v = values[0]
        for i in range(1, len(values)):
            v = jnp.where(k == i, values[i], v)
        return v

    def forward(k, _):
        for i, at_step in enumerate((0, 2, 3, 6)):
            @pl.when(k == at_step)
            def _():
                loads[i].wait()

        q = pick(k, (opp, opp, right, left, right, left, my, my))
        part = pick(k, (0, 1, 1, 0, 0, 1, 0, 1))
        some = pl.ds(pl.multiple_of(q * rows + part * half, half), half)
        pre = dot(xv[some], w_in[...])
        sig = jax.nn.sigmoid(pre)
        hidden = (pre * sig).astype(BF16)
        hv[some] = hidden
        dv[some] = sig * (1.0 + pre * (1.0 - sig))
        ypv[some] = dot(hidden, w_out[...])

        @pl.when(k == 1)
        def _():
            def sel_body(g, _):
                base = pl.multiple_of(g * 32, 32)
                r = lax.broadcasted_iota(jnp.int32, (32, 128), 0) + base
                for lc in range(recv // 128):
                    lanes = slice(lc * 128, lc * 128 + 128)
                    one = jnp.broadcast_to(rows_of[0:1, lanes], (32, 128))
                    low = jnp.where(one == r, 1.0, 0.0).astype(BF16)
                    high = jnp.where(one == r + half, 1.0, 0.0).astype(BF16)
                    ot[pl.ds(base, 32), lanes] = low
                    ot[pl.ds(base + half, 32), lanes] = high
                    ot2[pl.ds(base, 32), lanes] = low + high
                return 0

            lax.fori_loop(0, half // 32, sel_body, 0)

        @pl.when(k == 2)
        def _():
            pl.semaphore_wait(barrier, n_dp - 1 + n_mp - 1)
            r_a.start()
            l_a.start()
            bsend[0] = part_of(ypv, right, 1)[...].astype(BF16)

        @pl.when(k == 3)
        def _():
            bsend[1] = part_of(ypv, left, 0)[...].astype(BF16)

        return 0

    lax.fori_loop(0, 8, forward, 0)

    s_all, c_all = src[...], weight[...] * mask[...].astype(F32)
    total = c_all
    for k in range(1, pairs):
        hit = pltpu.roll(s_all, k, 0) == s_all
        total = total + jnp.where(hit, pltpu.roll(c_all, k, 0), 0.0)
    cw[...] = total.astype(BF16)
    s16[...] = s_all.astype(jnp.int16)

    span = 64

    def pair_chunk(lc):
        lanes = slice(lc * 128, lc * 128 + 128)
        s_l, c_l = s16[:, lanes], cw[:, lanes]
        ss = [jnp.broadcast_to(s_l[p : p + 1], (span, 128)) for p in range(pairs)]
        cs = [jnp.broadcast_to(c_l[p : p + 1], (span, 128)) for p in range(pairs)]

        def body(g, _):
            base = pl.multiple_of(g * span, span)
            r = (lax.broadcasted_iota(jnp.int32, (span, 128), 0) + base).astype(jnp.int16)
            acc = jnp.zeros((span, 128), BF16)
            for p in range(pairs):
                acc = jnp.where(ss[p] == r, cs[p], acc)
            at[pl.ds(base, span), lanes] = acc
            return 0

        lax.fori_loop(0, recv // span, body, 0)

    chunks = rows // 128
    for lc in range(chunks // 4):
        pair_chunk(lc)
    r_a.wait_recv()
    bsend[2] = (abuf[0] + part_of(ypv, right, 0)[...]).astype(BF16)
    r_c.start()
    l_a.wait_recv()
    bsend[3] = (abuf[1] + part_of(ypv, left, 1)[...]).astype(BF16)
    l_c.start()
    r_b.start()
    l_b.start()
    for lc in range(chunks // 4, chunks):
        pair_chunk(lc)
    for c in (r_b, l_b, r_c, l_c):
        c.wait_recv()
    y = (
        ypv[pl.ds(pl.multiple_of(my * rows, rows), rows)]
        + bbuf[0].reshape(rows, width).astype(F32)
        + bbuf[1].reshape(rows, width).astype(F32)
    )
    ybf[...] = y.astype(BF16)
    y_b = ybf[...]
    y_t = jnp.transpose(y_b.astype(F32)).astype(BF16)
    gram = dot(y_t, y_b)

    def group_device(k):
        return (k // NC * NX + xi) * NC + k % NC

    def sum_start(which, value):
        g_send[which] = value.reshape(ng, 8, width)
        g_in[which, gidx] = g_send[which, gidx]

        @pl.loop(1, ng)
        def _(k):
            peer = (gidx + k) % ng
            remote(g_send.at[which, peer], g_in.at[which, gidx], ar_s.at[which, 0], ar_r.at[which, 0], (group_device(peer), my)).start()

    def sum_x(which):
        drain(g_in.at[which, pl.ds(0, ng - 1)], ar_r.at[which, 0])
        t = g_in[which, 0]
        for k in range(1, ng):
            t = t + g_in[which, k]
        g_x[which, xi] = t
        for k in range(1, NX):
            peer = (zi * NX + (xi + k) % NX) * NC + ci
            remote(g_x.at[which, xi], g_x.at[which, xi], ar_s.at[which, 1], ar_r.at[which, 1], (peer, my)).start()

    def sum_y(which):
        drain(g_x.at[which, pl.ds(0, NX - 1)], ar_r.at[which, 1])
        t = g_x[which, 0]
        for k in range(1, NX):
            t = t + g_x[which, k]
        g_y[which, my] = t
        for k in range(1, n_mp):
            remote(g_y.at[which, my], g_y.at[which, my], ar_s.at[which, 2], ar_r.at[which, 2], (me, (my + k) % n_mp)).start()

    def sum_back(which):
        drain(g_y.at[which, pl.ds(0, n_mp - 1)], ar_r.at[which, 2])
        t = g_y[which, 0]
        for k in range(1, n_mp):
            t = t + g_y[which, k]
        g_all[which, gidx] = t

        @pl.loop(1, ng)
        def _(k):
            peer = (gidx + k) % ng
            remote(g_all.at[which, gidx], g_all.at[which, gidx], ar_s.at[which, 3], ar_r.at[which, 3], (group_device(peer), my)).start()

    def sum_end(which):
        drain(g_all.at[which, pl.ds(0, ng - 1)], ar_r.at[which, 3])
        return g_all[which].reshape(width, width) * (1.0 / nodes)

    sum_start(0, gram)

    far = tuple(sorted(range(nz), key=lambda k: -min(k, nz - k)))
    layer = NX * NC

    def send_layer(source, target, i, zc):
        for j in range(layer):
            peer = zc * layer + j

            @pl.when(peer != me)
            def _():
                remote(
                    source.at[pl.ds(pl.multiple_of(peer * slots, slots), slots)],
                    target.at[pl.ds(pl.multiple_of(me * slots, slots), slots)],
                    x_s.at[i], x_r.at[i], (peer, my),
                ).start()

    mine = pl.ds(pl.multiple_of(me * slots, slots), slots)
    wide = layer * slots
    y_t2 = jnp.concatenate([y_t[:, :half], y_t[:, half:]], axis=0)

    def gather_body(k, _):
        zc = (zi + pick(k, far)) % nz
        lanes = pl.ds(pl.multiple_of(zc * wide, wide), wide)
        both = dot(y_t2, ot2[:, lanes])
        rows_k = jnp.where(jnp.broadcast_to(rows_of[0:1, lanes] < half, (width, wide)), both[:width], both[width:])
        sbuf[lanes] = jnp.transpose(rows_k).astype(BF16)
        send_layer(sbuf, rbuf, 0, zc)
        return 0

    lax.fori_loop(0, nz, gather_body, 0)
    rbuf[mine] = sbuf[mine]
    sum_x(0)

    y_ones = jnp.concatenate([y_b, jnp.ones((rows, width), BF16)], axis=1)

    def aty_body(k, _):
        some = pl.ds(pl.multiple_of(k * 256, 256), 256)
        both = dot(at[some], y_ones)
        aty[some] = both
        whole = both[:, width:].astype(BF16).astype(F32)
        for j in range(2):
            d_send[2 * k + j] = jnp.transpose(whole[j * 128 : j * 128 + 128])[0:1]
        return 0

    lax.fori_loop(0, recv // 256, aty_body, 0)
    per = 128 // slots
    sum_y(0)

    @pl.loop(1, n_dp)
    def _(k):
        peer = (me + k) % n_dp
        remote(d_send.at[peer // per], d_in.at[me], x_s.at[2], x_r.at[2], (peer, my)).start()

    d_in[me] = d_send[me // per]
    sum_back(0)
    ones_r = jnp.ones((width, recv), BF16)

    def deg_body(k, _):
        lanes = pl.ds(pl.multiple_of(k * 256, 256), 256)
        degs[lanes] = jnp.transpose(dot(ones_r, at[:, lanes]))
        return 0

    lax.fori_loop(0, rows // 256, deg_body, 0)

    gram_n = sum_end(0)
    w[...] = gram_n
    lane = lax.broadcasted_iota(jnp.int32, (width, width), 1)
    sub = lax.broadcasted_iota(jnp.int32, (width, width), 0)

    def sweep(i, _):
        k = pl.multiple_of(2 * i, 2)
        a = w[...]
        r0, r1 = w[pl.ds(k, 1), :], w[pl.ds(k + 1, 1), :]
        m0, m1 = lane == k, lane == k + 1
        c0 = jnp.sum(jnp.where(m0, a, 0.0), axis=1, keepdims=True)
        c1 = jnp.sum(jnp.where(m1, a, 0.0), axis=1, keepdims=True)
        p = jnp.sum(jnp.where(m0[0:1], r0, 0.0), axis=1, keepdims=True)
        q = jnp.sum(jnp.where(m1[0:1], r0, 0.0), axis=1, keepdims=True)
        d = jnp.sum(jnp.where(m1[0:1], r1, 0.0), axis=1, keepdims=True)
        ip = 1.0 / p
        f = q * ip
        e11 = 1.0 / (d - q * f)
        e01 = -f * e11
        e00 = ip - f * e01
        t0, t1 = e00 * r0 + e01 * r1, e01 * r0 + e11 * r1
        new = a - (c0 * t0 + c1 * t1)
        new = jnp.where(m0, e00 * c0 + e01 * c1, jnp.where(m1, e01 * c0 + e11 * c1, new))
        w[...] = new
        w[pl.ds(k, 1), :] = jnp.where(m0[0:1], -e00, jnp.where(m1[0:1], -e01, t0))
        w[pl.ds(k + 1, 1), :] = jnp.where(m0[0:1], -e01, jnp.where(m1[0:1], -e11, t1))
        return 0

    steps = width // 2
    early = steps // 4
    lax.fori_loop(0, early, sweep, 0)

    drain(rbuf.at[pl.ds(0, recv - slots)], x_r.at[0])
    r_t = jnp.transpose(rbuf[...].astype(F32)).astype(BF16)

    order2 = (2, nz - 2) + tuple(k for k in far if k not in (2, nz - 2))

    def back_body(k, _):
        zc = (zi + pick(k, order2)) % nz
        some = pl.ds(pl.multiple_of(zc * wide, wide), wide)
        both = aty[some]
        cross, d_whole = both[:, :width], both[:, width:]
        r_k = rbuf[some].astype(F32)
        b_hi, b_lo = split(d_whole * r_k - cross)
        hib[some] = b_hi
        lob[some] = b_lo
        d_k = d_whole.astype(BF16).astype(F32)
        tbuf[some] = (cross - (d_whole - d_k) * r_k).astype(BF16)

        @pl.when(k < 2)
        def _():
            send_layer(tbuf, qbuf, 1, zc)

        return 0

    lax.fori_loop(0, nz, back_body, 0)

    def own_body(k, _):
        lanes = pl.ds(pl.multiple_of(k * 256, 256), 256)
        cross = jnp.transpose(dot(r_t, at[:, lanes]))
        own[lanes] = degs[lanes] * ybf[lanes].astype(F32) - cross
        return 0

    lax.fori_loop(0, rows // 256, own_body, 0)
    o_hi, o_lo = split(own[...])
    s_part = dot(y_t, o_hi) + dot(y_t, o_lo) + dot(r_t, hib[...]) + dot(r_t, lob[...])
    sum_start(1, s_part)

    def return_body(k, _):
        send_layer(tbuf, qbuf, 1, (zi + pick(k, order2)) % nz)
        return 0

    lax.fori_loop(2, nz, return_body, 0)
    qbuf[mine] = tbuf[mine]

    third = (steps - early) // 3
    lax.fori_loop(early, early + third, sweep, 0)
    sum_x(1)
    lax.fori_loop(early + third, early + 2 * third, sweep, 0)
    sum_y(1)
    lax.fori_loop(early + 2 * third, steps, sweep, 0)
    sum_back(1)
    drain(d_in.at[pl.ds(0, n_dp - 1)], x_r.at[2])
    d_all[...] = pltpu.roll(d_in[...].reshape(n_dp, 128), (128 - slots * (me % per)) % 128, 1)
    spot = lax.broadcasted_iota(jnp.int32, (recv // 128, 128), 1) // slots
    d_row = jnp.zeros((recv // 128, 128), F32)
    for j in range(per):
        piece = d_all[pl.ds(j, recv // 128, stride=per), :]
        d_row = jnp.where(spot == j, pltpu.roll(piece, slots * j, 1), d_row)
    for k in range(recv // 128):
        column = jnp.transpose(jnp.broadcast_to(d_row[k : k + 1], (128, width)))
        qd[k * 128 : k * 128 + 128, width:] = column.astype(BF16)
    inv0 = -w[...]
    eye2 = jnp.where(lane == sub, 2.0, 0.0)
    inverse = dot(inv0, eye2 - dot(gram_n, inv0, precision=HIGH), precision=HIGH)
    i_hi, i_lo = split(inverse * factor)
    i_both = jnp.concatenate([i_hi, i_lo], axis=1)
    s_n = sum_end(1)
    b0 = dot(inverse, s_n, precision=HIGH)
    b1 = b0 + dot(inverse, s_n - dot(gram_n, b0, precision=HIGH), precision=HIGH)
    b_hi = b1.astype(BF16)
    rest = b1 - b_hi.astype(F32)
    b_mid = rest.astype(BF16)
    b_lo = (rest - b_mid.astype(F32)).astype(BF16)
    b_low = jnp.concatenate([b_mid, b_lo], axis=1)

    def remove_body(k, _):
        some = pl.ds(pl.multiple_of(k * 256, 256), 256)
        yk = ybf[some]
        low = dot(yk, b_low)
        own[some] = own[some] - (dot(yk, b_hi) + (low[:, :width] + low[:, width:]))
        return 0

    lax.fori_loop(0, rows // 256, remove_body, 0)
    drain(qbuf.at[pl.ds(0, recv - slots)], x_r.at[1])

    qd[:, :width] = qbuf[...]
    gathers = []
    for i, (q, part, to) in enumerate(
        ((my, 0, right), (my, 1, left), (my, 1, right), (my, 0, left), (left, 0, right), (right, 1, left))
    ):
        gathers.append(remote(part_of(pc, q, part), part_of(pc, q, part), ag_s.at[i], ag_r.at[i], (me, to)))

    def grad_body(k, _):
        some = pl.ds(pl.multiple_of(k * 256, 256), 256)
        theirs = dot(ot[some], qd[...])
        n_hi, n_lo = split(own[some] + (theirs[:, width:] * ybf[some].astype(F32) - theirs[:, :width]))
        both = dot(n_hi, i_both)
        gy = both[:, :width] + (both[:, width:] + dot(n_lo, i_hi))
        pc[pl.ds(pl.multiple_of(my * rows + k * 256, 256), 256)] = gy.astype(BF16)

        @pl.when(k == half // 256 - 1)
        def _():
            gathers[0].start()

        return 0

    lax.fori_loop(0, rows // 256, grad_body, 0)
    for c in gathers[1:4]:
        c.start()
    gacc[...] = jnp.zeros_like(gacc)
    oacc[...] = jnp.zeros_like(oacc)

    def backward(k, _):
        for i, (at_step, then) in enumerate(((2, 4), (3, 5), (4, None), (5, None), (6, None), (7, None))):
            @pl.when(k == at_step)
            def _():
                gathers[i].wait_recv()
                if then is not None:
                    gathers[then].start()

        q = pick(k, (my, my, left, right, left, right, opp, opp))
        part = pick(k, (0, 1, 0, 1, 1, 0, 0, 1))
        some = pl.ds(pl.multiple_of(q * rows + part * half, half), half)
        gy = pc[some]
        dh = dot(gy, w_out[...], ((1,), (1,)))
        gp_t = jnp.transpose(dh * dv[some]).astype(BF16)
        gacc[...] += dot(gp_t, xv[some])
        oacc[...] += dot(jnp.transpose(gy.astype(F32)).astype(BF16), hv[some])
        return 0

    lax.fori_loop(0, 8, backward, 0)
    gi[...] = jnp.transpose(gacc[...])
    go[...] = jnp.transpose(oacc[...])

    x, z, c = xi, zi, ci

    def at_x(k):
        return ((z * NX + k) * NC + c, my)

    def at_z(k):
        return ((k * NX + x) * NC + c, my)

    mate = (me - c + (1 - c), my)
    hi, ho = xi_s.shape[0], xo_s.shape[0]
    qi, qo = hi // NX, ho // NX
    ti = qi // nz
    theirs_i = pl.ds(pl.multiple_of((1 - c) * hi, hi), hi)
    theirs_o = pl.ds(pl.multiple_of((1 - c) * ho, ho), ho)
    mine_i = pl.ds(pl.multiple_of(c * hi, hi), hi)
    mine_o = pl.ds(pl.multiple_of(c * ho, ho), ho)
    c_i = remote(gi.at[theirs_i], ci_r, s_s.at[0], s_r.at[0], mate)
    c_o = remote(go.at[theirs_o], co_r, s_s.at[1], s_r.at[1], mate)
    c_i.start()
    c_o.start()
    c_i.wait_recv()
    c_o.wait_recv()
    ci_r[...] = gi[mine_i] + ci_r[...]
    co_r[...] = go[mine_o] + co_r[...]
    xi_s[...] = ci_r[...].astype(BF16)
    xo_s[...] = co_r[...].astype(BF16)
    sent = [c_i, c_o]
    xs = []
    for k in (2, 1, 3):
        p = (x + k) % NX
        a = remote(xi_s.at[pl.ds(pl.multiple_of(p * qi, qi), qi)], xi_r.at[k - 1], s_s.at[2 * k], s_r.at[2 * k], at_x(p))
        b = remote(xo_s.at[pl.ds(pl.multiple_of(p * qo, qo), qo)], xo_r.at[k - 1], s_s.at[2 * k + 1], s_r.at[2 * k + 1], at_x(p))
        a.start()
        b.start()
        xs += [a, b]
    for d in xs:
        d.wait_recv()
    sent += xs
    t_i = ci_r[pl.ds(pl.multiple_of(x * qi, qi), qi)]
    t_o = co_r[pl.ds(pl.multiple_of(x * qo, qo), qo)]
    for k in range(NX - 1):
        t_i = t_i + xi_r[k].astype(F32)
        t_o = t_o + xo_r[k].astype(F32)
    zi_s[...] = t_i.astype(BF16)
    zo_s[...] = t_o.reshape(zo_s.shape)
    zo_r[z] = zo_s[z]
    zi_r[z] = zi_s[pl.ds(pl.multiple_of(z * ti, ti), ti)]
    order = sorted(range(1, nz), key=lambda k: -min(k, nz - k))
    for k in order:
        p = (z + k) % nz
        remote(zi_s.at[pl.ds(pl.multiple_of(p * ti, ti), ti)], zi_r.at[z], b_s.at[0], b_r.at[0], at_z(p)).start()
        remote(zo_s.at[p], zo_r.at[z], b_s.at[1], b_r.at[1], at_z(p)).start()

    drain(zi_r.at[pl.ds(0, nz - 1)], b_r.at[0])
    f_i = zi_r[0].astype(F32)
    for k in range(1, nz):
        f_i = f_i + zi_r[k].astype(F32)
    block_i = pl.ds(pl.multiple_of(c * hi + x * qi + z * ti, ti), ti)
    all_i[block_i] = f_i.astype(BF16)
    for k in order:
        remote(all_i.at[block_i], all_i.at[block_i], b_s.at[2], b_r.at[2], at_z((z + k) % nz)).start()
    drain(zo_r.at[pl.ds(0, nz - 1)], b_r.at[1])
    f_o = zo_r[0]
    for k in range(1, nz):
        f_o = f_o + zo_r[k]
    zo_a[z] = f_o
    for k in order:
        remote(zo_a.at[z], zo_a.at[z], b_s.at[7], b_r.at[7], at_z((z + k) % nz)).start()
    drain(zi_s.at[pl.ds(0, (nz - 1) * ti)], b_r.at[2])
    drain(zo_a.at[pl.ds(0, nz - 1)], b_r.at[7])
    quarter_o = pl.ds(pl.multiple_of(c * ho + x * qo, qo), qo)
    all_o[quarter_o] = zo_a[...].reshape(qo, width).astype(BF16)
    quarter_i = pl.ds(pl.multiple_of(c * hi + x * qi, qi), qi)
    for k in (2, 1, 3):
        remote(all_i.at[quarter_i], all_i.at[quarter_i], b_s.at[4], b_r.at[4], at_x((x + k) % NX)).start()
        remote(all_o.at[quarter_o], all_o.at[quarter_o], b_s.at[3], b_r.at[3], at_x((x + k) % NX)).start()
    drain(xo_s.at[pl.ds(0, (NX - 1) * qo)], b_r.at[3])
    d_o = remote(all_o.at[mine_o], all_o.at[mine_o], b_s.at[5], b_r.at[5], mate)
    d_o.start()
    drain(xi_s.at[pl.ds(0, (NX - 1) * qi)], b_r.at[4])
    d_i = remote(all_i.at[mine_i], all_i.at[mine_i], b_s.at[6], b_r.at[6], mate)
    d_i.start()
    for which in range(2):
        drain(g_send.at[which, pl.ds(0, ng - 1)], ar_s.at[which, 0])
        drain(g_x.at[which, pl.ds(0, NX - 1)], ar_s.at[which, 1])
        drain(g_y.at[which, pl.ds(0, n_mp - 1)], ar_s.at[which, 2])
        drain(g_all.at[which, pl.ds(0, ng - 1)], ar_s.at[which, 3])
    for d in gathers + [r_a, l_a, r_b, l_b, r_c, l_c]:
        d.wait_send()
    drain(sbuf.at[pl.ds(0, recv - slots)], x_s.at[0])
    drain(tbuf.at[pl.ds(0, recv - slots)], x_s.at[1])
    drain(d_in.at[pl.ds(0, n_dp - 1)], x_s.at[2])
    drain(zi_r.at[pl.ds(0, nz - 1)], b_s.at[0])
    drain(zo_r.at[pl.ds(0, nz - 1)], b_s.at[1])
    drain(zi_s.at[pl.ds(0, (nz - 1) * ti)], b_s.at[2])
    drain(zo_a.at[pl.ds(0, nz - 1)], b_s.at[7])
    drain(xo_s.at[pl.ds(0, (NX - 1) * qo)], b_s.at[3])
    drain(xi_s.at[pl.ds(0, (NX - 1) * qi)], b_s.at[4])
    for d in sent + [d_o, d_i]:
        d.wait_send()
    d_o.wait_recv()
    d_i.wait_recv()


def whole(features, w_in, w_out, src_t, weight_t, mask_t, send_row, n_dp, n_mp, nodes, factor):
    group, depth = features.shape
    units, width = w_out.shape
    rows = group // n_mp
    recv = send_row.shape[1]
    pairs = src_t.shape[0]
    nz = n_dp // (NX * NC)
    ng = n_dp // NX
    hi, ho = depth // NC, units // NC
    qi, qo = hi // NX, ho // NX
    vm = pltpu.VMEM
    dma = pltpu.SemaphoreType.DMA
    return pl.pallas_call(
        functools.partial(kernel, n_dp, n_mp, nodes, factor),
        out_shape=(jax.ShapeDtypeStruct((depth, units), BF16), jax.ShapeDtypeStruct((units, width), BF16)),
        in_specs=[pl.BlockSpec(memory_space=pl.ANY)] + [pl.BlockSpec(memory_space=vm)] * 6,
        out_specs=[pl.BlockSpec(memory_space=vm)] * 2,
        scratch_shapes=[
            vm((group, depth), BF16), vm((group, units), BF16), vm((group, units), F32), vm((group, width), F32),
            vm((rows, recv), BF16), vm((rows // 2, recv), BF16), vm((recv, rows), BF16), vm((pairs, rows), jnp.int16), vm((pairs, rows), BF16),
            vm((2, rows // 2, width), F32), vm((4, rows // 2, width), BF16), vm((2, 2, rows // 2, width), BF16),
            vm((rows, width), BF16),
            vm((recv, width), BF16), vm((recv, width), BF16), vm((recv, width), BF16), vm((recv, width), BF16),
            vm((recv, 2 * width), F32), vm((rows, width), F32), vm((rows, width), F32),
            vm((recv, width), BF16), vm((recv, width), BF16), vm((recv, 2 * width), BF16),
            vm((recv // 128, 1, 128), F32), vm((n_dp, 1, 128), F32), vm((n_dp, 128), F32),
            vm((group, width), BF16), vm((units, depth), F32), vm((width, units), F32),
            vm((depth, units), F32), vm((units, width), F32),
            vm((2, ng, 8, width), F32), vm((2, ng, 8, width), F32), vm((2, NX, 8, width), F32),
            vm((2, n_mp, 8, width), F32), vm((2, ng, 8, width), F32), vm((width, width), F32),
            vm((hi, units), F32), vm((ho, width), F32), vm((hi, units), BF16), vm((ho, width), BF16),
            vm((NX - 1, qi, units), BF16), vm((NX - 1, qo, width), BF16),
            vm((qi, units), BF16), vm((nz, qo // nz, width), F32), vm((nz, qi // nz, units), BF16), vm((nz, qo // nz, width), F32),
            vm((nz, qo // nz, width), F32),
            dma((4,)), dma((6,)), dma((6,)), dma((3,)), dma((3,)), dma((2, 4)), dma((2, 4)), dma((6,)), dma((6,)),
            dma((8,)), dma((8,)), dma((8,)), dma((8,)),
        ],
        compiler_params=pltpu.CompilerParams(collective_id=0, has_side_effects=True, vmem_limit_bytes=58 << 20),
        name="step",
    )(features, w_in, w_out, src_t, weight_t, mask_t, send_row)


def widen_kernel(a, b, oa, ob):
    oa[...] = a[...].astype(F32)
    ob[...] = b[...].astype(F32)


def widen(a, b):
    vm = pl.BlockSpec(memory_space=pltpu.VMEM)
    return pl.pallas_call(
        widen_kernel,
        out_shape=(jax.ShapeDtypeStruct(a.shape, F32), jax.ShapeDtypeStruct(b.shape, F32)),
        in_specs=[vm] * 2,
        out_specs=[vm] * 2,
        name="widen",
    )(a, b)


def shards(features, w_in, w_out, send_rows, pair_src, pair_weight, pair_mask):
    n_dp = lax.axis_size("dp")
    n_mp = lax.axis_size("mp")
    nodes = features.shape[0] * n_dp
    pairs = pair_src.shape[1]
    scale = 1.0 / (pairs * math.sqrt(nodes))
    return widen(
        *whole(
            features, w_in, w_out, pair_src.T, pair_weight.T, pair_mask.T, send_rows.reshape(1, -1),
            n_dp, n_mp, nodes, 2.0 * scale,
        )
    )


def solution(mesh):
    return jax.shard_map(
        shards,
        mesh=mesh,
        in_specs=(
            P("dp", None),
            P(None, "mp"),
            P("mp", None),
            P(("dp", "mp")),
            P(("dp", "mp"), None),
            P(("dp", "mp"), None),
            P(("dp", "mp"), None),
        ),
        out_specs=(P(None, "mp"), P("mp", None)),
        check_vma=False,
    )
```

```python
import functools
import math

import jax
import jax.numpy as jnp
from jax import lax
from jax.experimental import pallas as pl
from jax.experimental.pallas import tpu as pltpu
from jax.sharding import PartitionSpec as P

MESH = pl.DeviceIdType.MESH
HIGH = lax.Precision.HIGHEST
F32 = jnp.float32
BF16 = jnp.bfloat16
NX = 4
NC = 2


def dot(a, b, dims=((1,), (0,)), precision=None):
    return lax.dot_general(a, b, (dims, ((), ())), precision=precision, preferred_element_type=F32)


def split(v):
    hi = v.astype(BF16)
    return hi, (v - hi.astype(F32)).astype(BF16)


def remote(src, dst, ssem, rsem, where):
    return pltpu.make_async_remote_copy(
        src_ref=src, dst_ref=dst, send_sem=ssem, recv_sem=rsem, device_id=where, device_id_type=MESH
    )


def drain(view, sem):
    pltpu.make_async_copy(view, view, sem).wait()


def kernel(
    n_dp, n_mp, nodes, factor,
    x_hbm, w_in, w_out, src, weight, mask, rows_of, all_i, all_o,
    xv, hv, dv, ypv, ot, ot2, at, s16, cw, abuf, bsend, bbuf, ybf, sbuf, rbuf, tbuf, qbuf, aty, degs, own, hib, lob, dcol,
    d_send, d_in, d_all, pc, gacc, oacc, gi, go,
    g_send, g_in, g_xy, g_all, w,
    ci_r, co_r, xi_s, xo_s, xi_r, xo_r, zi_s, zo_s, zi_r, zo_r, zo_a,
    ld_s, rs_s, rs_r, x_s, d_s, x_r, ar_s, ar_r, ag_s, ag_r, s_s, s_r, b_s, b_r,
):
    me = lax.axis_index("dp")
    my = lax.axis_index("mp")
    nz = n_dp // (NX * NC)
    ng = nz * NC
    zi, xi, ci = me // (NX * NC), me // NC % NX, me % NC
    gidx = zi * NC + ci
    pidx = xi * n_mp + my
    right, left, opp = (my + 1) % n_mp, (my + n_mp - 1) % n_mp, (my + 2) % n_mp
    rows, width = ybf.shape
    half = rows // 2
    recv = rbuf.shape[0]
    slots = recv // n_dp
    pairs = src.shape[0]

    def load(i, q):
        some = pl.ds(pl.multiple_of(q * rows, rows), rows)
        return pltpu.make_async_copy(x_hbm.at[some], xv.at[some], ld_s.at[i])

    loads = [load(i, q) for i, q in enumerate((opp, right, left, my))]
    for c in loads:
        c.start()

    barrier = pltpu.get_barrier_semaphore()

    @pl.loop(1, n_dp)
    def _(k):
        pl.semaphore_signal(barrier, inc=1, device_id=((me + k) % n_dp, my), device_id_type=MESH)

    @pl.loop(1, n_mp)
    def _(k):
        pl.semaphore_signal(barrier, inc=1, device_id=(me, (my + k) % n_mp), device_id_type=MESH)

    for dx in range(1, NX):
        for dy in range(1, n_mp):
            other = (zi * NX + (xi + dx) % NX) * NC + ci
            pl.semaphore_signal(barrier, inc=1, device_id=(other, (my + dy) % n_mp), device_id_type=MESH)

    def part_of(ref, q, part):
        return ref.at[pl.ds(pl.multiple_of(q * rows + part * half, half), half)]

    r_a = remote(bsend.at[4], abuf.at[0], rs_s.at[0], rs_r.at[0], (me, right))
    l_a = remote(bsend.at[5], abuf.at[1], rs_s.at[1], rs_r.at[1], (me, left))
    r_b = remote(bsend.at[0], bbuf.at[0, 1], rs_s.at[2], rs_r.at[2], (me, right))
    l_b = remote(bsend.at[1], bbuf.at[1, 0], rs_s.at[3], rs_r.at[3], (me, left))
    r_c = remote(bsend.at[2], bbuf.at[0, 0], rs_s.at[4], rs_r.at[4], (me, right))
    l_c = remote(bsend.at[3], bbuf.at[1, 1], rs_s.at[5], rs_r.at[5], (me, left))

    def pick(k, values):
        v = values[0]
        for i in range(1, len(values)):
            v = jnp.where(k == i, values[i], v)
        return v

    def forward(k, _):
        for i, at_step in enumerate((0, 2, 3, 6)):
            @pl.when(k == at_step)
            def _():
                loads[i].wait()

        q = pick(k, (opp, opp, right, left, right, left, my, my))
        part = pick(k, (0, 1, 1, 0, 0, 1, 0, 1))
        some = pl.ds(pl.multiple_of(q * rows + part * half, half), half)
        pre = dot(xv[some], w_in[...])
        sig = jax.nn.sigmoid(pre)
        hidden = (pre * sig).astype(BF16)
        hv[some] = hidden
        dv[some] = sig * (1.0 + pre * (1.0 - sig))
        ypv[some] = dot(hidden, w_out[...])

        @pl.when(k == 1)
        def _():
            def sel_body(g, _):
                base = pl.multiple_of(g * 32, 32)
                r = lax.broadcasted_iota(jnp.int32, (32, 128), 0) + base
                for lc in range(recv // 128):
                    lanes = slice(lc * 128, lc * 128 + 128)
                    one = jnp.broadcast_to(rows_of[0:1, lanes], (32, 128))
                    low = jnp.where(one == r, 1.0, 0.0).astype(BF16)
                    high = jnp.where(one == r + half, 1.0, 0.0).astype(BF16)
                    ot[pl.ds(base, 32), lanes] = low
                    ot[pl.ds(base + half, 32), lanes] = high
                    ot2[pl.ds(base, 32), lanes] = low + high
                return 0

            lax.fori_loop(0, half // 32, sel_body, 0)

        @pl.when(k == 2)
        def _():
            pl.semaphore_wait(barrier, n_dp - 1 + n_mp - 1 + (NX - 1) * (n_mp - 1))
            bsend[4] = part_of(ypv, opp, 0)[...].astype(BF16)
            bsend[5] = part_of(ypv, opp, 1)[...].astype(BF16)
            r_a.start()
            l_a.start()
            bsend[0] = part_of(ypv, right, 1)[...].astype(BF16)
            r_b.start()

        @pl.when(k == 3)
        def _():
            bsend[1] = part_of(ypv, left, 0)[...].astype(BF16)
            l_b.start()

        return 0

    lax.fori_loop(0, 8, forward, 0)

    s_all, c_all = src[...], weight[...] * mask[...].astype(F32)
    total = c_all
    for k in range(1, pairs):
        hit = pltpu.roll(s_all, k, 0) == s_all
        total = total + jnp.where(hit, pltpu.roll(c_all, k, 0), 0.0)
    cw[...] = total.astype(BF16)
    s16[...] = s_all.astype(jnp.int16)

    span = 64

    def pair_chunk(lc):
        lanes = slice(lc * 128, lc * 128 + 128)
        s_l, c_l = s16[:, lanes], cw[:, lanes]
        ss = [jnp.broadcast_to(s_l[p : p + 1], (span, 128)) for p in range(pairs)]
        cs = [jnp.broadcast_to(c_l[p : p + 1], (span, 128)) for p in range(pairs)]

        def body(g, _):
            base = pl.multiple_of(g * span, span)
            r = (lax.broadcasted_iota(jnp.int32, (span, 128), 0) + base).astype(jnp.int16)
            acc = jnp.zeros((span, 128), BF16)
            for p in range(pairs):
                acc = jnp.where(ss[p] == r, cs[p], acc)
            at[pl.ds(base, span), lanes] = acc
            return 0

        lax.fori_loop(0, recv // span, body, 0)

    chunks = rows // 128
    for lc in range(3 * chunks // 8):
        pair_chunk(lc)
    r_a.wait_recv()
    bsend[2] = (abuf[0].astype(F32) + part_of(ypv, right, 0)[...]).astype(BF16)
    r_c.start()
    l_a.wait_recv()
    bsend[3] = (abuf[1].astype(F32) + part_of(ypv, left, 1)[...]).astype(BF16)
    l_c.start()
    for lc in range(3 * chunks // 8, chunks):
        pair_chunk(lc)
    ones_r = jnp.ones((width, recv), BF16)

    def deg_body(k, _):
        lanes = pl.ds(pl.multiple_of(k * 256, 256), 256)
        degs[lanes] = jnp.transpose(dot(ones_r, at[:, lanes]))
        return 0

    lax.fori_loop(0, rows // 256, deg_body, 0)

    for c in (r_b, l_b, r_c, l_c):
        c.wait_recv()
    y = (
        ypv[pl.ds(pl.multiple_of(my * rows, rows), rows)]
        + bbuf[0].reshape(rows, width).astype(F32)
        + bbuf[1].reshape(rows, width).astype(F32)
    )
    ybf[...] = y.astype(BF16)
    y_b = ybf[...]
    y_t = jnp.transpose(y_b.astype(F32)).astype(BF16)
    gram = dot(y_t, y_b)

    def group_device(k):
        return (k // NC * NX + xi) * NC + k % NC

    def sum_start(which, value):
        g_send[which] = value.reshape(ng, 8, width)
        g_in[which, gidx] = g_send[which, gidx]

        @pl.loop(1, ng)
        def _(k):
            peer = (gidx + k) % ng
            remote(g_send.at[which, peer], g_in.at[which, gidx], ar_s.at[which, 0], ar_r.at[which, 0], (group_device(peer), my)).start()

    def plane_device(k):
        return (zi * NX + k // n_mp) * NC + ci, k % n_mp

    def sum_plane(which):
        drain(g_in.at[which, pl.ds(0, ng - 1)], ar_r.at[which, 0])
        t = g_in[which, 0]
        for k in range(1, ng):
            t = t + g_in[which, k]
        g_xy[which, pidx] = t

        @pl.loop(1, NX * n_mp)
        def _(k):
            remote(g_xy.at[which, pidx], g_xy.at[which, pidx], ar_s.at[which, 1], ar_r.at[which, 1], plane_device((pidx + k) % (NX * n_mp))).start()

    def sum_back(which):
        drain(g_xy.at[which, pl.ds(0, NX * n_mp - 1)], ar_r.at[which, 1])
        t = g_xy[which, 0]
        for k in range(1, NX * n_mp):
            t = t + g_xy[which, k]
        g_all[which, gidx] = t

        @pl.loop(1, ng)
        def _(k):
            peer = (gidx + k) % ng
            remote(g_all.at[which, gidx], g_all.at[which, gidx], ar_s.at[which, 2], ar_r.at[which, 2], (group_device(peer), my)).start()

    def sum_end(which):
        drain(g_all.at[which, pl.ds(0, ng - 1)], ar_r.at[which, 2])
        return g_all[which].reshape(width, width) * (1.0 / nodes)

    sum_start(0, gram)

    turns = [(nz // 2,)] + [(k, nz - k) for k in range(nz // 2 - 1, 0, -1)] + [(0,)]
    layer = NX * NC
    wide = layer * slots

    def layer_rows(k):
        return pl.ds(pl.multiple_of((zi + k) % nz * wide, wide), wide)

    def send_layer(source, target, i, k):
        zc = (zi + k) % nz
        for j in range(layer):
            peer = zc * layer + j

            def send():
                remote(
                    source.at[pl.ds(pl.multiple_of(peer * slots, slots), slots)],
                    target.at[pl.ds(pl.multiple_of(me * slots, slots), slots)],
                    x_s.at[i, k], x_r.at[i], (peer, my),
                ).start()

            if k:
                send()
            else:
                pl.when(peer != me)(send)

    def sent_layer(source, i, k):
        drain(source.at[pl.ds(0, wide if k else wide - slots)], x_s.at[i, k])

    mine = pl.ds(pl.multiple_of(me * slots, slots), slots)
    y_t2 = jnp.concatenate([y_t[:, :half], y_t[:, half:]], axis=0)
    y_ones = jnp.concatenate([y_b, jnp.ones((rows, width), BF16)], axis=1)

    def gather_layer(k):
        lanes = layer_rows(k)
        both = dot(y_t2, ot2[:, lanes])
        rows_k = jnp.where(jnp.broadcast_to(rows_of[0:1, lanes] < half, (width, wide)), both[:width], both[width:])
        sbuf[lanes] = jnp.transpose(rows_k).astype(BF16)

    def weigh_layer(k):
        some = pl.ds(k * wide, wide)
        both = dot(at[some], y_ones)
        aty[some] = both
        tbuf[some] = both[:, :width].astype(BF16)
        for j in range(wide // 128):
            d_send[wide // 128 * k + j] = jnp.transpose(both[j * 128 : j * 128 + 128, width:])[0:1]

    def send_turn(i, t):
        last = (i, t - 2) if t >= 2 else (i - 1, len(turns) + t - 2)
        if last[0] >= 0:
            for k in turns[last[1]]:
                sent_layer((sbuf, tbuf)[last[0]], last[0], k)
        for k in turns[t]:
            send_layer((sbuf, tbuf)[i], (rbuf, qbuf)[i], i, k)

    weighed = 0
    for t, turn in enumerate(turns):
        for k in turn:
            gather_layer(k)
        send_turn(0, t)
        for _ in range(2 if t < 3 else 1):
            weigh_layer(weighed)
            weighed += 1
        if t == 2:
            sum_plane(0)
    rbuf[mine] = sbuf[mine]
    qbuf[mine] = tbuf[mine]
    sum_back(0)
    send_turn(1, 0)
    send_turn(1, 1)
    drain(rbuf.at[pl.ds(0, recv - slots)], x_r.at[0])
    r_t = jnp.transpose(rbuf[...].astype(F32)).astype(BF16)

    def back_body(k, _):
        some = pl.ds(pl.multiple_of(k * wide, wide), wide)
        both = aty[some]
        b_hi, b_lo = split(both[:, width:] * rbuf[some].astype(F32) - both[:, :width])
        hib[some] = b_hi
        lob[some] = b_lo
        return 0

    lax.fori_loop(0, nz, back_body, 0)

    def own_body(k, _):
        lanes = pl.ds(pl.multiple_of(k * 256, 256), 256)
        cross = jnp.transpose(dot(r_t, at[:, lanes]))
        own[lanes] = degs[lanes] * ybf[lanes].astype(F32) - cross
        return 0

    lax.fori_loop(0, rows // 256, own_body, 0)
    o_hi, o_lo = split(own[...])
    s_part = dot(y_t, o_hi) + dot(y_t, o_lo) + dot(r_t, hib[...]) + dot(r_t, lob[...])
    sum_start(1, s_part)

    send_turn(1, 2)

    per = 128 // slots

    @pl.loop(1, n_dp)
    def _(k):
        peer = (me + k) % n_dp
        remote(d_send.at[peer // per], d_in.at[me], d_s, x_r.at[2], (peer, my)).start()

    d_in[me] = d_send[me // per]
    gram_n = sum_end(0)
    w[...] = gram_n
    lane = lax.broadcasted_iota(jnp.int32, (width, width), 1)
    sub = lax.broadcasted_iota(jnp.int32, (width, width), 0)

    def sweep(i, _):
        k = pl.multiple_of(2 * i, 2)
        a = w[...]
        r0, r1 = w[pl.ds(k, 1), :], w[pl.ds(k + 1, 1), :]
        m0, m1 = lane == k, lane == k + 1
        c0 = jnp.sum(jnp.where(m0, a, 0.0), axis=1, keepdims=True)
        c1 = jnp.sum(jnp.where(m1, a, 0.0), axis=1, keepdims=True)
        p = jnp.sum(jnp.where(m0[0:1], r0, 0.0), axis=1, keepdims=True)
        q = jnp.sum(jnp.where(m1[0:1], r0, 0.0), axis=1, keepdims=True)
        d = jnp.sum(jnp.where(m1[0:1], r1, 0.0), axis=1, keepdims=True)
        ip = 1.0 / p
        f = q * ip
        e11 = 1.0 / (d - q * f)
        e01 = -f * e11
        e00 = ip - f * e01
        t0, t1 = e00 * r0 + e01 * r1, e01 * r0 + e11 * r1
        new = a - (c0 * t0 + c1 * t1)
        new = jnp.where(m0, e00 * c0 + e01 * c1, jnp.where(m1, e01 * c0 + e11 * c1, new))
        w[...] = new
        w[pl.ds(k, 1), :] = jnp.where(m0[0:1], -e00, jnp.where(m1[0:1], -e01, t0))
        w[pl.ds(k + 1, 1), :] = jnp.where(m0[0:1], -e01, jnp.where(m1[0:1], -e11, t1))
        return 0

    steps = width // 2

    fifth = steps // 5

    def sweeps(t):
        lax.fori_loop(t * fifth, steps if t == 4 else (t + 1) * fifth, sweep, 0)

    sweeps(0)
    sweeps(1)
    send_turn(1, 3)
    sweeps(2)
    sum_plane(1)
    sweeps(3)
    send_turn(1, 4)
    sweeps(4)
    sum_back(1)
    drain(d_in.at[pl.ds(0, n_dp - 1)], x_r.at[2])
    d_all[...] = pltpu.roll(d_in[...].reshape(n_dp, 128), (128 - slots * (me % per)) % 128, 1)
    spot = lax.broadcasted_iota(jnp.int32, (recv // 128, 128), 1) // slots
    d_row = jnp.zeros((recv // 128, 128), F32)
    for j in range(per):
        piece = d_all[pl.ds(j, recv // 128, stride=per), :]
        d_row = jnp.where(spot == j, pltpu.roll(piece, slots * j, 1), d_row)
    for k in range(recv // 128):
        column = jnp.transpose(jnp.broadcast_to(d_row[k : k + 1], (128, width)))
        d_hi, d_lo = split(column)
        dcol[k * 128 : k * 128 + 128] = jnp.where(lane < width // 2, d_hi.astype(F32), d_lo.astype(F32)).astype(BF16)

    def add_body(k, _):
        some = pl.ds(pl.multiple_of(k * 256, 256), 256)
        extra = dot(ot[some], dcol[...])
        own[some] = own[some] + (extra[:, 0:1] + extra[:, width - 1 :]) * ybf[some].astype(F32)
        return 0

    lax.fori_loop(0, rows // 256, add_body, 0)
    inv0 = -w[...]
    eye2 = jnp.where(lane == sub, 2.0, 0.0)
    inverse = dot(inv0, eye2 - dot(gram_n, inv0, precision=HIGH), precision=HIGH)
    i_hi, i_lo = split(inverse * factor)
    i_both = jnp.concatenate([i_hi, i_lo], axis=1)
    s_n = sum_end(1)
    b0 = dot(inverse, s_n, precision=HIGH)
    b1 = b0 + dot(inverse, s_n - dot(gram_n, b0, precision=HIGH), precision=HIGH)
    b_hi = b1.astype(BF16)
    rest = b1 - b_hi.astype(F32)
    b_mid = rest.astype(BF16)
    b_lo = (rest - b_mid.astype(F32)).astype(BF16)
    b_low = jnp.concatenate([b_mid, b_lo], axis=1)

    def remove_body(k, _):
        some = pl.ds(pl.multiple_of(k * 256, 256), 256)
        yk = ybf[some]
        low = dot(yk, b_low)
        own[some] = own[some] - (dot(yk, b_hi) + (low[:, :width] + low[:, width:]))
        return 0

    lax.fori_loop(0, rows // 256, remove_body, 0)
    drain(qbuf.at[pl.ds(0, recv - slots)], x_r.at[1])

    gathers = []
    for i, (q, part, to) in enumerate(
        ((my, 0, right), (my, 1, left), (my, 1, right), (my, 0, left), (left, 0, right), (right, 1, left))
    ):
        gathers.append(remote(part_of(pc, q, part), part_of(pc, q, part), ag_s.at[i], ag_r.at[i], (me, to)))

    def grad_body(k, _):
        some = pl.ds(pl.multiple_of(k * 256, 256), 256)
        n_hi, n_lo = split(own[some] - dot(ot[some], qbuf[...]))
        both = dot(n_hi, i_both)
        gy = both[:, :width] + (both[:, width:] + dot(n_lo, i_hi))
        pc[pl.ds(pl.multiple_of(my * rows + k * 256, 256), 256)] = gy.astype(BF16)

        @pl.when(k == half // 256 - 1)
        def _():
            gathers[0].start()

        return 0

    lax.fori_loop(0, rows // 256, grad_body, 0)
    for c in gathers[1:4]:
        c.start()
    gacc[...] = jnp.zeros_like(gacc)
    oacc[...] = jnp.zeros_like(oacc)

    def backward(k, _):
        for i, (at_step, then) in enumerate(((2, 4), (3, 5), (4, None), (5, None), (6, None), (7, None))):
            @pl.when(k == at_step)
            def _():
                gathers[i].wait_recv()
                if then is not None:
                    gathers[then].start()

        q = pick(k, (my, my, left, right, left, right, opp, opp))
        part = pick(k, (0, 1, 0, 1, 1, 0, 0, 1))
        some = pl.ds(pl.multiple_of(q * rows + part * half, half), half)
        gy = pc[some]
        dh = dot(gy, w_out[...], ((1,), (1,)))
        gp_t = jnp.transpose(dh * dv[some]).astype(BF16)
        gacc[...] += dot(gp_t, xv[some])
        oacc[...] += dot(jnp.transpose(gy.astype(F32)).astype(BF16), hv[some])
        return 0

    lax.fori_loop(0, 8, backward, 0)
    gi[...] = jnp.transpose(gacc[...])
    go[...] = jnp.transpose(oacc[...])

    x, z, c = xi, zi, ci

    def at_x(k):
        return ((z * NX + k) * NC + c, my)

    def at_z(k):
        return ((k * NX + x) * NC + c, my)

    mate = (me - c + (1 - c), my)
    hi, ho = xi_s.shape[0], xo_s.shape[0]
    qi, qo = hi // NX, ho // NX
    ti = qi // nz
    theirs_i = pl.ds(pl.multiple_of((1 - c) * hi, hi), hi)
    theirs_o = pl.ds(pl.multiple_of((1 - c) * ho, ho), ho)
    mine_i = pl.ds(pl.multiple_of(c * hi, hi), hi)
    mine_o = pl.ds(pl.multiple_of(c * ho, ho), ho)
    c_i = remote(gi.at[theirs_i], ci_r, s_s.at[0], s_r.at[0], mate)
    c_o = remote(go.at[theirs_o], co_r, s_s.at[1], s_r.at[1], mate)
    c_i.start()
    c_o.start()
    c_i.wait_recv()
    c_o.wait_recv()
    ci_r[...] = gi[mine_i] + ci_r[...]
    co_r[...] = go[mine_o] + co_r[...]
    xi_s[...] = ci_r[...].astype(BF16)
    xo_s[...] = co_r[...].astype(BF16)
    sent = [c_i, c_o]
    xs = []
    for k in (2, 1, 3):
        p = (x + k) % NX
        a = remote(xi_s.at[pl.ds(pl.multiple_of(p * qi, qi), qi)], xi_r.at[k - 1], s_s.at[2 * k], s_r.at[2 * k], at_x(p))
        b = remote(xo_s.at[pl.ds(pl.multiple_of(p * qo, qo), qo)], xo_r.at[k - 1], s_s.at[2 * k + 1], s_r.at[2 * k + 1], at_x(p))
        a.start()
        b.start()
        xs += [a, b]
    for d in xs:
        d.wait_recv()
    sent += xs
    t_i = ci_r[pl.ds(pl.multiple_of(x * qi, qi), qi)]
    t_o = co_r[pl.ds(pl.multiple_of(x * qo, qo), qo)]
    for k in range(NX - 1):
        t_i = t_i + xi_r[k].astype(F32)
        t_o = t_o + xo_r[k].astype(F32)
    zi_s[...] = t_i.astype(BF16)
    zo_s[...] = t_o.reshape(zo_s.shape)
    zo_r[z] = zo_s[z]
    zi_r[z] = zi_s[pl.ds(pl.multiple_of(z * ti, ti), ti)]
    order = sorted(range(1, nz), key=lambda k: -min(k, nz - k))
    for k in order:
        p = (z + k) % nz
        remote(zi_s.at[pl.ds(pl.multiple_of(p * ti, ti), ti)], zi_r.at[z], b_s.at[0], b_r.at[0], at_z(p)).start()
        remote(zo_s.at[p], zo_r.at[z], b_s.at[1], b_r.at[1], at_z(p)).start()

    drain(zi_r.at[pl.ds(0, nz - 1)], b_r.at[0])
    f_i = zi_r[0].astype(F32)
    for k in range(1, nz):
        f_i = f_i + zi_r[k].astype(F32)
    block_i = pl.ds(pl.multiple_of(c * hi + x * qi + z * ti, ti), ti)
    all_i[block_i] = f_i.astype(BF16)
    for k in order:
        remote(all_i.at[block_i], all_i.at[block_i], b_s.at[2], b_r.at[2], at_z((z + k) % nz)).start()
    drain(zo_r.at[pl.ds(0, nz - 1)], b_r.at[1])
    f_o = zo_r[0]
    for k in range(1, nz):
        f_o = f_o + zo_r[k]
    zo_a[z] = f_o
    for k in order:
        remote(zo_a.at[z], zo_a.at[z], b_s.at[7], b_r.at[7], at_z((z + k) % nz)).start()
    drain(zi_s.at[pl.ds(0, (nz - 1) * ti)], b_r.at[2])
    drain(zo_a.at[pl.ds(0, nz - 1)], b_r.at[7])
    quarter_o = pl.ds(pl.multiple_of(c * ho + x * qo, qo), qo)
    all_o[quarter_o] = zo_a[...].reshape(qo, width).astype(BF16)
    quarter_i = pl.ds(pl.multiple_of(c * hi + x * qi, qi), qi)
    for k in (2, 1, 3):
        remote(all_i.at[quarter_i], all_i.at[quarter_i], b_s.at[4], b_r.at[4], at_x((x + k) % NX)).start()
        remote(all_o.at[quarter_o], all_o.at[quarter_o], b_s.at[3], b_r.at[3], at_x((x + k) % NX)).start()
    drain(xo_s.at[pl.ds(0, (NX - 1) * qo)], b_r.at[3])
    d_o = remote(all_o.at[mine_o], all_o.at[mine_o], b_s.at[5], b_r.at[5], mate)
    d_o.start()
    drain(xi_s.at[pl.ds(0, (NX - 1) * qi)], b_r.at[4])
    d_i = remote(all_i.at[mine_i], all_i.at[mine_i], b_s.at[6], b_r.at[6], mate)
    d_i.start()
    for which in range(2):
        drain(g_send.at[which, pl.ds(0, ng - 1)], ar_s.at[which, 0])
        drain(g_xy.at[which, pl.ds(0, NX * n_mp - 1)], ar_s.at[which, 1])
        drain(g_all.at[which, pl.ds(0, ng - 1)], ar_s.at[which, 2])
    for d in gathers + [r_a, l_a, r_b, l_b, r_c, l_c]:
        d.wait_send()
    for t in (-2, -1):
        for k in turns[t]:
            sent_layer(tbuf, 1, k)
    drain(d_in.at[pl.ds(0, n_dp - 1)], d_s)
    drain(zi_r.at[pl.ds(0, nz - 1)], b_s.at[0])
    drain(zo_r.at[pl.ds(0, nz - 1)], b_s.at[1])
    drain(zi_s.at[pl.ds(0, (nz - 1) * ti)], b_s.at[2])
    drain(zo_a.at[pl.ds(0, nz - 1)], b_s.at[7])
    drain(xo_s.at[pl.ds(0, (NX - 1) * qo)], b_s.at[3])
    drain(xi_s.at[pl.ds(0, (NX - 1) * qi)], b_s.at[4])
    for d in sent + [d_o, d_i]:
        d.wait_send()
    d_o.wait_recv()
    d_i.wait_recv()


def whole(features, w_in, w_out, src_t, weight_t, mask_t, send_row, n_dp, n_mp, nodes, factor):
    group, depth = features.shape
    units, width = w_out.shape
    rows = group // n_mp
    recv = send_row.shape[1]
    pairs = src_t.shape[0]
    nz = n_dp // (NX * NC)
    ng = n_dp // NX
    hi, ho = depth // NC, units // NC
    qi, qo = hi // NX, ho // NX
    vm = pltpu.VMEM
    dma = pltpu.SemaphoreType.DMA
    return pl.pallas_call(
        functools.partial(kernel, n_dp, n_mp, nodes, factor),
        out_shape=(jax.ShapeDtypeStruct((depth, units), BF16), jax.ShapeDtypeStruct((units, width), BF16)),
        in_specs=[pl.BlockSpec(memory_space=pl.ANY)] + [pl.BlockSpec(memory_space=vm)] * 6,
        out_specs=[pl.BlockSpec(memory_space=vm)] * 2,
        scratch_shapes=[
            vm((group, depth), BF16), vm((group, units), BF16), vm((group, units), F32), vm((group, width), F32),
            vm((rows, recv), BF16), vm((rows // 2, recv), BF16), vm((recv, rows), BF16), vm((pairs, rows), jnp.int16), vm((pairs, rows), BF16),
            vm((2, rows // 2, width), BF16), vm((6, rows // 2, width), BF16), vm((2, 2, rows // 2, width), BF16),
            vm((rows, width), BF16),
            vm((recv, width), BF16), vm((recv, width), BF16), vm((recv, width), BF16), vm((recv, width), BF16),
            vm((recv, 2 * width), F32), vm((rows, width), F32), vm((rows, width), F32),
            vm((recv, width), BF16), vm((recv, width), BF16), vm((recv, width), BF16),
            vm((recv // 128, 1, 128), F32), vm((n_dp, 1, 128), F32), vm((n_dp, 128), F32),
            vm((group, width), BF16), vm((units, depth), F32), vm((width, units), F32),
            vm((depth, units), F32), vm((units, width), F32),
            vm((2, ng, 8, width), F32), vm((2, ng, 8, width), F32), vm((2, NX * n_mp, 8, width), F32),
            vm((2, ng, 8, width), F32), vm((width, width), F32),
            vm((hi, units), F32), vm((ho, width), F32), vm((hi, units), BF16), vm((ho, width), BF16),
            vm((NX - 1, qi, units), BF16), vm((NX - 1, qo, width), BF16),
            vm((qi, units), BF16), vm((nz, qo // nz, width), F32), vm((nz, qi // nz, units), BF16), vm((nz, qo // nz, width), F32),
            vm((nz, qo // nz, width), F32),
            dma((4,)), dma((6,)), dma((6,)), dma((2, nz)), dma, dma((3,)), dma((2, 3)), dma((2, 3)), dma((6,)), dma((6,)),
            dma((8,)), dma((8,)), dma((8,)), dma((8,)),
        ],
        compiler_params=pltpu.CompilerParams(collective_id=0, has_side_effects=True, vmem_limit_bytes=58 << 20),
        name="step",
    )(features, w_in, w_out, src_t, weight_t, mask_t, send_row)


def widen_kernel(a, b, oa, ob):
    oa[...] = a[...].astype(F32)
    ob[...] = b[...].astype(F32)


def widen(a, b):
    vm = pl.BlockSpec(memory_space=pltpu.VMEM)
    return pl.pallas_call(
        widen_kernel,
        out_shape=(jax.ShapeDtypeStruct(a.shape, F32), jax.ShapeDtypeStruct(b.shape, F32)),
        in_specs=[vm] * 2,
        out_specs=[vm] * 2,
        name="widen",
    )(a, b)


def shards(features, w_in, w_out, send_rows, pair_src, pair_weight, pair_mask):
    n_dp = lax.axis_size("dp")
    n_mp = lax.axis_size("mp")
    nodes = features.shape[0] * n_dp
    pairs = pair_src.shape[1]
    scale = 1.0 / (pairs * math.sqrt(nodes))
    return widen(
        *whole(
            features, w_in, w_out, pair_src.T, pair_weight.T, pair_mask.T, send_rows.reshape(1, -1),
            n_dp, n_mp, nodes, 2.0 * scale,
        )
    )


def solution(mesh):
    return jax.shard_map(
        shards,
        mesh=mesh,
        in_specs=(
            P("dp", None),
            P(None, "mp"),
            P("mp", None),
            P(("dp", "mp")),
            P(("dp", "mp"), None),
            P(("dp", "mp"), None),
            P(("dp", "mp"), None),
        ),
        out_specs=(P(None, "mp"), P("mp", None)),
        check_vma=False,
    )
```

```python
import functools
import math

import jax
import jax.numpy as jnp
from jax import lax
from jax.experimental import pallas as pl
from jax.experimental.pallas import tpu as pltpu
from jax.sharding import PartitionSpec as P

MESH = pl.DeviceIdType.MESH
HIGH = lax.Precision.HIGHEST
F32 = jnp.float32
BF16 = jnp.bfloat16
NX = 4
NC = 2


def dot(a, b, dims=((1,), (0,)), precision=None):
    return lax.dot_general(a, b, (dims, ((), ())), precision=precision, preferred_element_type=F32)


def split(v):
    hi = v.astype(BF16)
    return hi, (v - hi.astype(F32)).astype(BF16)


def remote(src, dst, ssem, rsem, where):
    return pltpu.make_async_remote_copy(
        src_ref=src, dst_ref=dst, send_sem=ssem, recv_sem=rsem, device_id=where, device_id_type=MESH
    )


def drain(view, sem):
    pltpu.make_async_copy(view, view, sem).wait()


def kernel(
    n_dp, n_mp, nodes, factor,
    x_hbm, w_in, w_out, src, weight, mask, rows_of, all_i, all_o,
    xv, hv, dv, ypv, ot, ot2, at, s16, cw, abuf, bsend, bbuf, ybf, sbuf, rbuf, tbuf, qbuf, aty, degs, own, hib, lob, clo, dcol,
    d_send, d_in, d_all, pc, gacc, oacc, gi, go,
    g_send, g_in, g_xy, g_all, w,
    ci_r, co_r, xi_s, xo_s, xi_r, xo_r, zi_s, zo_s, zi_r, zo_r, zo_a,
    ld_s, rs_s, rs_r, x_s, d_s, x_r, ar_s, ar_r, ag_s, ag_r, s_s, s_r, b_s, b_r,
):
    me = lax.axis_index("dp")
    my = lax.axis_index("mp")
    nz = n_dp // (NX * NC)
    ng = nz * NC
    zi, xi, ci = me // (NX * NC), me // NC % NX, me % NC
    gidx = zi * NC + ci
    pidx = xi * n_mp + my
    right, left, opp = (my + 1) % n_mp, (my + n_mp - 1) % n_mp, (my + 2) % n_mp
    rows, width = ybf.shape
    half = rows // 2
    recv = rbuf.shape[0]
    slots = recv // n_dp
    pairs = src.shape[0]

    def load(i, q):
        some = pl.ds(pl.multiple_of(q * rows, rows), rows)
        return pltpu.make_async_copy(x_hbm.at[some], xv.at[some], ld_s.at[i])

    loads = [load(i, q) for i, q in enumerate((opp, right, left, my))]
    for c in loads:
        c.start()

    barrier = pltpu.get_barrier_semaphore()

    @pl.loop(1, n_dp)
    def _(k):
        pl.semaphore_signal(barrier, inc=1, device_id=((me + k) % n_dp, my), device_id_type=MESH)

    @pl.loop(1, n_mp)
    def _(k):
        pl.semaphore_signal(barrier, inc=1, device_id=(me, (my + k) % n_mp), device_id_type=MESH)

    for dx in range(1, NX):
        for dy in range(1, n_mp):
            other = (zi * NX + (xi + dx) % NX) * NC + ci
            pl.semaphore_signal(barrier, inc=1, device_id=(other, (my + dy) % n_mp), device_id_type=MESH)

    def part_of(ref, q, part):
        return ref.at[pl.ds(pl.multiple_of(q * rows + part * half, half), half)]

    r_a = remote(bsend.at[4], abuf.at[0], rs_s.at[0], rs_r.at[0], (me, right))
    l_a = remote(bsend.at[5], abuf.at[1], rs_s.at[1], rs_r.at[1], (me, left))
    r_b = remote(bsend.at[0], bbuf.at[0, 1], rs_s.at[2], rs_r.at[2], (me, right))
    l_b = remote(bsend.at[1], bbuf.at[1, 0], rs_s.at[3], rs_r.at[3], (me, left))
    r_c = remote(bsend.at[2], bbuf.at[0, 0], rs_s.at[4], rs_r.at[4], (me, right))
    l_c = remote(bsend.at[3], bbuf.at[1, 1], rs_s.at[5], rs_r.at[5], (me, left))

    def pick(k, values):
        v = values[0]
        for i in range(1, len(values)):
            v = jnp.where(k == i, values[i], v)
        return v

    def forward(k, _):
        for i, at_step in enumerate((0, 2, 3, 6)):
            @pl.when(k == at_step)
            def _():
                loads[i].wait()

        q = pick(k, (opp, opp, right, left, right, left, my, my))
        part = pick(k, (0, 1, 1, 0, 0, 1, 0, 1))
        some = pl.ds(pl.multiple_of(q * rows + part * half, half), half)
        pre = dot(xv[some], w_in[...])
        sig = jax.nn.sigmoid(pre)
        hidden = (pre * sig).astype(BF16)
        hv[some] = hidden
        dv[some] = sig * (1.0 + pre * (1.0 - sig))
        ypv[some] = dot(hidden, w_out[...])

        @pl.when(k == 1)
        def _():
            def sel_body(g, _):
                base = pl.multiple_of(g * 32, 32)
                r = lax.broadcasted_iota(jnp.int32, (32, 128), 0) + base
                for lc in range(recv // 128):
                    lanes = slice(lc * 128, lc * 128 + 128)
                    one = jnp.broadcast_to(rows_of[0:1, lanes], (32, 128))
                    low = jnp.where(one == r, 1.0, 0.0).astype(BF16)
                    high = jnp.where(one == r + half, 1.0, 0.0).astype(BF16)
                    ot[pl.ds(base, 32), lanes] = low
                    ot[pl.ds(base + half, 32), lanes] = high
                    ot2[pl.ds(base, 32), lanes] = low + high
                return 0

            lax.fori_loop(0, half // 32, sel_body, 0)

        @pl.when(k == 2)
        def _():
            pl.semaphore_wait(barrier, n_dp - 1 + n_mp - 1 + (NX - 1) * (n_mp - 1))
            bsend[4] = part_of(ypv, opp, 0)[...].astype(BF16)
            bsend[5] = part_of(ypv, opp, 1)[...].astype(BF16)
            r_a.start()
            l_a.start()
            bsend[0] = part_of(ypv, right, 1)[...].astype(BF16)
            r_b.start()

        @pl.when(k == 3)
        def _():
            bsend[1] = part_of(ypv, left, 0)[...].astype(BF16)
            l_b.start()

        return 0

    lax.fori_loop(0, 8, forward, 0)

    s_all, c_all = src[...], weight[...] * mask[...].astype(F32)
    total = c_all
    for k in range(1, pairs):
        hit = pltpu.roll(s_all, k, 0) == s_all
        total = total + jnp.where(hit, pltpu.roll(c_all, k, 0), 0.0)
    cw[...] = total.astype(BF16)
    s16[...] = s_all.astype(jnp.int16)

    span = 64

    def pair_chunk(lc):
        lanes = slice(lc * 128, lc * 128 + 128)
        s_l, c_l = s16[:, lanes], cw[:, lanes]
        ss = [jnp.broadcast_to(s_l[p : p + 1], (span, 128)) for p in range(pairs)]
        cs = [jnp.broadcast_to(c_l[p : p + 1], (span, 128)) for p in range(pairs)]

        def body(g, _):
            base = pl.multiple_of(g * span, span)
            r = (lax.broadcasted_iota(jnp.int32, (span, 128), 0) + base).astype(jnp.int16)
            acc = jnp.zeros((span, 128), BF16)
            for p in range(pairs):
                acc = jnp.where(ss[p] == r, cs[p], acc)
            at[pl.ds(base, span), lanes] = acc
            return 0

        lax.fori_loop(0, recv // span, body, 0)

    chunks = rows // 128
    for lc in range(3 * chunks // 8):
        pair_chunk(lc)
    r_a.wait_recv()
    bsend[2] = (abuf[0].astype(F32) + part_of(ypv, right, 0)[...]).astype(BF16)
    r_c.start()
    l_a.wait_recv()
    bsend[3] = (abuf[1].astype(F32) + part_of(ypv, left, 1)[...]).astype(BF16)
    l_c.start()
    late = chunks - 3
    for lc in range(3 * chunks // 8, late):
        pair_chunk(lc)
    for c in (r_b, l_b, r_c, l_c):
        c.wait_recv()
    y = (
        ypv[pl.ds(pl.multiple_of(my * rows, rows), rows)]
        + bbuf[0].reshape(rows, width).astype(F32)
        + bbuf[1].reshape(rows, width).astype(F32)
    )
    ybf[...] = y.astype(BF16)
    y_b = ybf[...]
    y_t = jnp.transpose(y_b.astype(F32)).astype(BF16)
    gram = dot(y_t, y_b)

    def group_device(k):
        return (k // NC * NX + xi) * NC + k % NC

    def sum_start(which, value):
        g_send[which] = value.reshape(ng, 8, width)
        g_in[which, gidx] = g_send[which, gidx]

        @pl.loop(1, ng)
        def _(k):
            peer = (gidx + k) % ng
            remote(g_send.at[which, peer], g_in.at[which, gidx], ar_s.at[which, 0], ar_r.at[which, 0], (group_device(peer), my)).start()

    def plane_device(k):
        return (zi * NX + k // n_mp) * NC + ci, k % n_mp

    def sum_plane(which):
        drain(g_in.at[which, pl.ds(0, ng - 1)], ar_r.at[which, 0])
        t = g_in[which, 0]
        for k in range(1, ng):
            t = t + g_in[which, k]
        g_xy[which, pidx] = t

        @pl.loop(1, NX * n_mp)
        def _(k):
            remote(g_xy.at[which, pidx], g_xy.at[which, pidx], ar_s.at[which, 1], ar_r.at[which, 1], plane_device((pidx + k) % (NX * n_mp))).start()

    def sum_back(which):
        drain(g_xy.at[which, pl.ds(0, NX * n_mp - 1)], ar_r.at[which, 1])
        t = g_xy[which, 0]
        for k in range(1, NX * n_mp):
            t = t + g_xy[which, k]
        g_all[which, gidx] = t

        @pl.loop(1, ng)
        def _(k):
            peer = (gidx + k) % ng
            remote(g_all.at[which, gidx], g_all.at[which, gidx], ar_s.at[which, 2], ar_r.at[which, 2], (group_device(peer), my)).start()

    def sum_end(which):
        drain(g_all.at[which, pl.ds(0, ng - 1)], ar_r.at[which, 2])
        return g_all[which].reshape(width, width) * (1.0 / nodes)

    sum_start(0, gram)

    turns = [(nz // 2,)] + [(k, nz - k) for k in range(nz // 2 - 1, 0, -1)] + [(0,)]
    layer = NX * NC
    wide = layer * slots

    def layer_rows(k):
        return pl.ds(pl.multiple_of((zi + k) % nz * wide, wide), wide)

    def send_layer(source, target, i, k):
        zc = (zi + k) % nz
        for j in range(layer):
            peer = zc * layer + j

            def send():
                remote(
                    source.at[pl.ds(pl.multiple_of(peer * slots, slots), slots)],
                    target.at[pl.ds(pl.multiple_of(me * slots, slots), slots)],
                    x_s.at[i, k], x_r.at[i], (peer, my),
                ).start()

            if k:
                send()
            else:
                pl.when(peer != me)(send)

    def sent_layer(source, i, k):
        drain(source.at[pl.ds(0, wide if k else wide - slots)], x_s.at[i, k])

    mine = pl.ds(pl.multiple_of(me * slots, slots), slots)
    y_t2 = jnp.concatenate([y_t[:, :half], y_t[:, half:]], axis=0)
    y_ones = jnp.concatenate([y_b, jnp.ones((rows, width), BF16)], axis=1)

    def gather_layer(k):
        lanes = layer_rows(k)
        both = dot(y_t2, ot2[:, lanes])
        rows_k = jnp.where(jnp.broadcast_to(rows_of[0:1, lanes] < half, (width, wide)), both[:width], both[width:])
        sbuf[lanes] = jnp.transpose(rows_k).astype(BF16)

    def weigh_layer(k):
        some = pl.ds(k * wide, wide)
        both = dot(at[some], y_ones)
        aty[some] = both
        c_hi, c_lo = split(both[:, :width])
        tbuf[some] = c_hi
        clo[some] = c_lo
        for j in range(wide // 128):
            d_send[wide // 128 * k + j] = jnp.transpose(both[j * 128 : j * 128 + 128, width:])[0:1]

    plan = [(0, t) for t in turns] + [(1, t) for t in (turns[2], turns[3], turns[4], turns[0], turns[1])]
    first = len(turns)

    def send_turn(n):
        if n >= 2:
            i, layers = plan[n - 2]
            for k in layers:
                sent_layer((sbuf, tbuf)[i], i, k)
        i, layers = plan[n]
        for k in layers:
            send_layer((sbuf, tbuf)[i], (rbuf, qbuf)[i], i, k)

    weighed = 0
    for t, turn in enumerate(turns):
        for k in turn:
            gather_layer(k)
        send_turn(t)
        if late + t < chunks:
            pair_chunk(late + t)
        for _ in range(0 if t < 2 else 3 if t < 4 else 2):
            weigh_layer(weighed)
            weighed += 1
        if t == 2:
            sum_plane(0)
    rbuf[mine] = sbuf[mine]
    qbuf[mine] = tbuf[mine]
    sum_back(0)
    send_turn(first)
    send_turn(first + 1)
    ones_r = jnp.ones((width, recv), BF16)

    def deg_body(k, _):
        lanes = pl.ds(pl.multiple_of(k * 256, 256), 256)
        degs[lanes] = jnp.transpose(dot(ones_r, at[:, lanes]))
        return 0

    lax.fori_loop(0, rows // 256, deg_body, 0)

    o_hi, o_lo = split(degs[...] * y_b.astype(F32))
    s_own = dot(y_t, o_hi) + dot(y_t, o_lo)

    drain(rbuf.at[pl.ds(0, recv - slots)], x_r.at[0])
    r_t = jnp.transpose(rbuf[...].astype(F32)).astype(BF16)

    def back_body(k, _):
        some = pl.ds(pl.multiple_of(k * wide, wide), wide)
        both = aty[some]
        b_hi, b_lo = split(both[:, width:] * rbuf[some].astype(F32) - both[:, :width])
        hib[some] = b_hi
        lob[some] = b_lo
        return 0

    lax.fori_loop(0, nz, back_body, 0)

    mixed = dot(r_t, tbuf[...]) + dot(r_t, clo[...])
    s_part = s_own + (dot(r_t, hib[...]) + dot(r_t, lob[...])) - jnp.transpose(mixed)
    sum_start(1, s_part)
    send_turn(first + 2)


    per = 128 // slots

    @pl.loop(1, n_dp)
    def _(k):
        peer = (me + k) % n_dp
        remote(d_send.at[peer // per], d_in.at[me], d_s, x_r.at[2], (peer, my)).start()

    d_in[me] = d_send[me // per]
    gram_n = sum_end(0)
    w[...] = gram_n
    lane = lax.broadcasted_iota(jnp.int32, (width, width), 1)
    sub = lax.broadcasted_iota(jnp.int32, (width, width), 0)

    def sweep(i, _):
        k = pl.multiple_of(2 * i, 2)
        a = w[...]
        r0, r1 = w[pl.ds(k, 1), :], w[pl.ds(k + 1, 1), :]
        m0, m1 = lane == k, lane == k + 1
        c0 = jnp.sum(jnp.where(m0, a, 0.0), axis=1, keepdims=True)
        c1 = jnp.sum(jnp.where(m1, a, 0.0), axis=1, keepdims=True)
        p = jnp.sum(jnp.where(m0[0:1], r0, 0.0), axis=1, keepdims=True)
        q = jnp.sum(jnp.where(m1[0:1], r0, 0.0), axis=1, keepdims=True)
        d = jnp.sum(jnp.where(m1[0:1], r1, 0.0), axis=1, keepdims=True)
        ip = 1.0 / p
        f = q * ip
        e11 = 1.0 / (d - q * f)
        e01 = -f * e11
        e00 = ip - f * e01
        t0, t1 = e00 * r0 + e01 * r1, e01 * r0 + e11 * r1
        new = a - (c0 * t0 + c1 * t1)
        new = jnp.where(m0, e00 * c0 + e01 * c1, jnp.where(m1, e01 * c0 + e11 * c1, new))
        w[...] = new
        w[pl.ds(k, 1), :] = jnp.where(m0[0:1], -e00, jnp.where(m1[0:1], -e01, t0))
        w[pl.ds(k + 1, 1), :] = jnp.where(m0[0:1], -e01, jnp.where(m1[0:1], -e11, t1))
        return 0

    steps = width // 2

    def own_body(k, _):
        lanes = pl.ds(pl.multiple_of(k * 256, 256), 256)
        cross = jnp.transpose(dot(r_t, at[:, lanes]))
        own[lanes] = degs[lanes] * ybf[lanes].astype(F32) - cross
        return 0

    lax.fori_loop(0, rows // 256, own_body, 0)
    fifth = steps // 5

    def sweeps(t):
        lax.fori_loop(t * fifth, steps if t == 4 else (t + 1) * fifth, sweep, 0)

    sweeps(0)
    send_turn(first + 3)
    sweeps(1)
    sweeps(2)
    sum_plane(1)
    send_turn(first + 4)
    sweeps(3)
    sweeps(4)
    sum_back(1)
    drain(d_in.at[pl.ds(0, n_dp - 1)], x_r.at[2])
    d_all[...] = pltpu.roll(d_in[...].reshape(n_dp, 128), (128 - slots * (me % per)) % 128, 1)
    spot = lax.broadcasted_iota(jnp.int32, (recv // 128, 128), 1) // slots
    d_row = jnp.zeros((recv // 128, 128), F32)
    for j in range(per):
        piece = d_all[pl.ds(j, recv // 128, stride=per), :]
        d_row = jnp.where(spot == j, pltpu.roll(piece, slots * j, 1), d_row)
    for k in range(recv // 128):
        column = jnp.transpose(jnp.broadcast_to(d_row[k : k + 1], (128, width)))
        d_hi, d_lo = split(column)
        dcol[k * 128 : k * 128 + 128] = jnp.where(lane < width // 2, d_hi.astype(F32), d_lo.astype(F32)).astype(BF16)

    def add_body(k, _):
        some = pl.ds(pl.multiple_of(k * 256, 256), 256)
        extra = dot(ot[some], dcol[...])
        own[some] = own[some] + (extra[:, 0:1] + extra[:, width - 1 :]) * ybf[some].astype(F32)
        return 0

    lax.fori_loop(0, rows // 256, add_body, 0)
    inv0 = -w[...]
    eye2 = jnp.where(lane == sub, 2.0, 0.0)
    inverse = dot(inv0, eye2 - dot(gram_n, inv0, precision=HIGH), precision=HIGH)
    i_hi, i_lo = split(inverse * factor)
    i_both = jnp.concatenate([i_hi, i_lo], axis=1)
    s_n = sum_end(1)
    b0 = dot(inverse, s_n, precision=HIGH)
    b1 = b0 + dot(inverse, s_n - dot(gram_n, b0, precision=HIGH), precision=HIGH)
    b_hi = b1.astype(BF16)
    rest = b1 - b_hi.astype(F32)
    b_mid = rest.astype(BF16)
    b_lo = (rest - b_mid.astype(F32)).astype(BF16)
    b_low = jnp.concatenate([b_mid, b_lo], axis=1)

    def remove_body(k, _):
        some = pl.ds(pl.multiple_of(k * 256, 256), 256)
        yk = ybf[some]
        low = dot(yk, b_low)
        own[some] = own[some] - (dot(yk, b_hi) + (low[:, :width] + low[:, width:]))
        return 0

    lax.fori_loop(0, rows // 256, remove_body, 0)
    drain(qbuf.at[pl.ds(0, recv - slots)], x_r.at[1])

    gathers = []
    for i, (q, part, to) in enumerate(
        ((my, 0, right), (my, 1, left), (my, 1, right), (my, 0, left), (left, 0, right), (right, 1, left))
    ):
        gathers.append(remote(part_of(pc, q, part), part_of(pc, q, part), ag_s.at[i], ag_r.at[i], (me, to)))

    def grad_body(k, _):
        some = pl.ds(pl.multiple_of(k * 256, 256), 256)
        n_hi, n_lo = split(own[some] - dot(ot[some], qbuf[...]))
        both = dot(n_hi, i_both)
        gy = both[:, :width] + (both[:, width:] + dot(n_lo, i_hi))
        pc[pl.ds(pl.multiple_of(my * rows + k * 256, 256), 256)] = gy.astype(BF16)

        @pl.when(k == half // 256 - 1)
        def _():
            gathers[0].start()

        return 0

    lax.fori_loop(0, rows // 256, grad_body, 0)
    for c in gathers[1:4]:
        c.start()
    gacc[...] = jnp.zeros_like(gacc)
    oacc[...] = jnp.zeros_like(oacc)

    def backward(k, _):
        for i, (at_step, then) in enumerate(((2, 4), (3, 5), (4, None), (5, None), (6, None), (7, None))):
            @pl.when(k == at_step)
            def _():
                gathers[i].wait_recv()
                if then is not None:
                    gathers[then].start()

        q = pick(k, (my, my, left, right, left, right, opp, opp))
        part = pick(k, (0, 1, 0, 1, 1, 0, 0, 1))
        some = pl.ds(pl.multiple_of(q * rows + part * half, half), half)
        gy = pc[some]
        dh = dot(gy, w_out[...], ((1,), (1,)))
        gp_t = jnp.transpose(dh * dv[some]).astype(BF16)
        gacc[...] += dot(gp_t, xv[some])
        oacc[...] += dot(jnp.transpose(gy.astype(F32)).astype(BF16), hv[some])
        return 0

    lax.fori_loop(0, 8, backward, 0)
    gi[...] = jnp.transpose(gacc[...])
    go[...] = jnp.transpose(oacc[...])

    x, z, c = xi, zi, ci

    def at_x(k):
        return ((z * NX + k) * NC + c, my)

    def at_z(k):
        return ((k * NX + x) * NC + c, my)

    mate = (me - c + (1 - c), my)
    hi, ho = xi_s.shape[0], xo_s.shape[0]
    qi, qo = hi // NX, ho // NX
    ti = qi // nz
    theirs_i = pl.ds(pl.multiple_of((1 - c) * hi, hi), hi)
    theirs_o = pl.ds(pl.multiple_of((1 - c) * ho, ho), ho)
    mine_i = pl.ds(pl.multiple_of(c * hi, hi), hi)
    mine_o = pl.ds(pl.multiple_of(c * ho, ho), ho)
    c_i = remote(gi.at[theirs_i], ci_r, s_s.at[0], s_r.at[0], mate)
    c_o = remote(go.at[theirs_o], co_r, s_s.at[1], s_r.at[1], mate)
    c_i.start()
    c_o.start()
    c_i.wait_recv()
    c_o.wait_recv()
    ci_r[...] = gi[mine_i] + ci_r[...]
    co_r[...] = go[mine_o] + co_r[...]
    xi_s[...] = ci_r[...].astype(BF16)
    xo_s[...] = co_r[...].astype(BF16)
    sent = [c_i, c_o]
    xs = []
    for k in (2, 1, 3):
        p = (x + k) % NX
        a = remote(xi_s.at[pl.ds(pl.multiple_of(p * qi, qi), qi)], xi_r.at[k - 1], s_s.at[2 * k], s_r.at[2 * k], at_x(p))
        b = remote(xo_s.at[pl.ds(pl.multiple_of(p * qo, qo), qo)], xo_r.at[k - 1], s_s.at[2 * k + 1], s_r.at[2 * k + 1], at_x(p))
        a.start()
        b.start()
        xs += [a, b]
    for d in xs:
        d.wait_recv()
    sent += xs
    t_i = ci_r[pl.ds(pl.multiple_of(x * qi, qi), qi)]
    t_o = co_r[pl.ds(pl.multiple_of(x * qo, qo), qo)]
    for k in range(NX - 1):
        t_i = t_i + xi_r[k].astype(F32)
        t_o = t_o + xo_r[k].astype(F32)
    zi_s[...] = t_i.astype(BF16)
    zo_s[...] = t_o.reshape(zo_s.shape)
    zo_r[z] = zo_s[z]
    zi_r[z] = zi_s[pl.ds(pl.multiple_of(z * ti, ti), ti)]
    order = sorted(range(1, nz), key=lambda k: -min(k, nz - k))
    for k in order:
        p = (z + k) % nz
        remote(zi_s.at[pl.ds(pl.multiple_of(p * ti, ti), ti)], zi_r.at[z], b_s.at[0], b_r.at[0], at_z(p)).start()
        remote(zo_s.at[p], zo_r.at[z], b_s.at[1], b_r.at[1], at_z(p)).start()

    drain(zi_r.at[pl.ds(0, nz - 1)], b_r.at[0])
    f_i = zi_r[0].astype(F32)
    for k in range(1, nz):
        f_i = f_i + zi_r[k].astype(F32)
    block_i = pl.ds(pl.multiple_of(c * hi + x * qi + z * ti, ti), ti)
    all_i[block_i] = f_i.astype(BF16)
    for k in order:
        remote(all_i.at[block_i], all_i.at[block_i], b_s.at[2], b_r.at[2], at_z((z + k) % nz)).start()
    drain(zo_r.at[pl.ds(0, nz - 1)], b_r.at[1])
    f_o = zo_r[0]
    for k in range(1, nz):
        f_o = f_o + zo_r[k]
    zo_a[z] = f_o
    for k in order:
        remote(zo_a.at[z], zo_a.at[z], b_s.at[7], b_r.at[7], at_z((z + k) % nz)).start()
    drain(zi_s.at[pl.ds(0, (nz - 1) * ti)], b_r.at[2])
    drain(zo_a.at[pl.ds(0, nz - 1)], b_r.at[7])
    quarter_o = pl.ds(pl.multiple_of(c * ho + x * qo, qo), qo)
    all_o[quarter_o] = zo_a[...].reshape(qo, width).astype(BF16)
    quarter_i = pl.ds(pl.multiple_of(c * hi + x * qi, qi), qi)
    for k in (2, 1, 3):
        remote(all_i.at[quarter_i], all_i.at[quarter_i], b_s.at[4], b_r.at[4], at_x((x + k) % NX)).start()
        remote(all_o.at[quarter_o], all_o.at[quarter_o], b_s.at[3], b_r.at[3], at_x((x + k) % NX)).start()
    drain(xo_s.at[pl.ds(0, (NX - 1) * qo)], b_r.at[3])
    d_o = remote(all_o.at[mine_o], all_o.at[mine_o], b_s.at[5], b_r.at[5], mate)
    d_o.start()
    drain(xi_s.at[pl.ds(0, (NX - 1) * qi)], b_r.at[4])
    d_i = remote(all_i.at[mine_i], all_i.at[mine_i], b_s.at[6], b_r.at[6], mate)
    d_i.start()
    for which in range(2):
        drain(g_send.at[which, pl.ds(0, ng - 1)], ar_s.at[which, 0])
        drain(g_xy.at[which, pl.ds(0, NX * n_mp - 1)], ar_s.at[which, 1])
        drain(g_all.at[which, pl.ds(0, ng - 1)], ar_s.at[which, 2])
    for d in gathers + [r_a, l_a, r_b, l_b, r_c, l_c]:
        d.wait_send()
    for i, layers in plan[-2:]:
        for k in layers:
            sent_layer(tbuf, i, k)
    drain(d_in.at[pl.ds(0, n_dp - 1)], d_s)
    drain(zi_r.at[pl.ds(0, nz - 1)], b_s.at[0])
    drain(zo_r.at[pl.ds(0, nz - 1)], b_s.at[1])
    drain(zi_s.at[pl.ds(0, (nz - 1) * ti)], b_s.at[2])
    drain(zo_a.at[pl.ds(0, nz - 1)], b_s.at[7])
    drain(xo_s.at[pl.ds(0, (NX - 1) * qo)], b_s.at[3])
    drain(xi_s.at[pl.ds(0, (NX - 1) * qi)], b_s.at[4])
    for d in sent + [d_o, d_i]:
        d.wait_send()
    d_o.wait_recv()
    d_i.wait_recv()


def whole(features, w_in, w_out, src_t, weight_t, mask_t, send_row, n_dp, n_mp, nodes, factor):
    group, depth = features.shape
    units, width = w_out.shape
    rows = group // n_mp
    recv = send_row.shape[1]
    pairs = src_t.shape[0]
    nz = n_dp // (NX * NC)
    ng = n_dp // NX
    hi, ho = depth // NC, units // NC
    qi, qo = hi // NX, ho // NX
    vm = pltpu.VMEM
    dma = pltpu.SemaphoreType.DMA
    return pl.pallas_call(
        functools.partial(kernel, n_dp, n_mp, nodes, factor),
        out_shape=(jax.ShapeDtypeStruct((depth, units), BF16), jax.ShapeDtypeStruct((units, width), BF16)),
        in_specs=[pl.BlockSpec(memory_space=pl.ANY)] + [pl.BlockSpec(memory_space=vm)] * 6,
        out_specs=[pl.BlockSpec(memory_space=vm)] * 2,
        scratch_shapes=[
            vm((group, depth), BF16), vm((group, units), BF16), vm((group, units), F32), vm((group, width), F32),
            vm((rows, recv), BF16), vm((rows // 2, recv), BF16), vm((recv, rows), BF16), vm((pairs, rows), jnp.int16), vm((pairs, rows), BF16),
            vm((2, rows // 2, width), BF16), vm((6, rows // 2, width), BF16), vm((2, 2, rows // 2, width), BF16),
            vm((rows, width), BF16),
            vm((recv, width), BF16), vm((recv, width), BF16), vm((recv, width), BF16), vm((recv, width), BF16),
            vm((recv, 2 * width), F32), vm((rows, width), F32), vm((rows, width), F32),
            vm((recv, width), BF16), vm((recv, width), BF16), vm((recv, width), BF16), vm((recv, width), BF16),
            vm((recv // 128, 1, 128), F32), vm((n_dp, 1, 128), F32), vm((n_dp, 128), F32),
            vm((group, width), BF16), vm((units, depth), F32), vm((width, units), F32),
            vm((depth, units), F32), vm((units, width), F32),
            vm((2, ng, 8, width), F32), vm((2, ng, 8, width), F32), vm((2, NX * n_mp, 8, width), F32),
            vm((2, ng, 8, width), F32), vm((width, width), F32),
            vm((hi, units), F32), vm((ho, width), F32), vm((hi, units), BF16), vm((ho, width), BF16),
            vm((NX - 1, qi, units), BF16), vm((NX - 1, qo, width), BF16),
            vm((qi, units), BF16), vm((nz, qo // nz, width), F32), vm((nz, qi // nz, units), BF16), vm((nz, qo // nz, width), F32),
            vm((nz, qo // nz, width), F32),
            dma((4,)), dma((6,)), dma((6,)), dma((2, nz)), dma, dma((3,)), dma((2, 3)), dma((2, 3)), dma((6,)), dma((6,)),
            dma((8,)), dma((8,)), dma((8,)), dma((8,)),
        ],
        compiler_params=pltpu.CompilerParams(collective_id=0, has_side_effects=True, vmem_limit_bytes=58 << 20),
        name="step",
    )(features, w_in, w_out, src_t, weight_t, mask_t, send_row)


def widen_kernel(a, b, oa, ob):
    oa[...] = a[...].astype(F32)
    ob[...] = b[...].astype(F32)


def widen(a, b):
    vm = pl.BlockSpec(memory_space=pltpu.VMEM)
    return pl.pallas_call(
        widen_kernel,
        out_shape=(jax.ShapeDtypeStruct(a.shape, F32), jax.ShapeDtypeStruct(b.shape, F32)),
        in_specs=[vm] * 2,
        out_specs=[vm] * 2,
        name="widen",
    )(a, b)


def shards(features, w_in, w_out, send_rows, pair_src, pair_weight, pair_mask):
    n_dp = lax.axis_size("dp")
    n_mp = lax.axis_size("mp")
    nodes = features.shape[0] * n_dp
    pairs = pair_src.shape[1]
    scale = 1.0 / (pairs * math.sqrt(nodes))
    return widen(
        *whole(
            features, w_in, w_out, pair_src.T, pair_weight.T, pair_mask.T, send_rows.reshape(1, -1),
            n_dp, n_mp, nodes, 2.0 * scale,
        )
    )


def solution(mesh):
    return jax.shard_map(
        shards,
        mesh=mesh,
        in_specs=(
            P("dp", None),
            P(None, "mp"),
            P("mp", None),
            P(("dp", "mp")),
            P(("dp", "mp"), None),
            P(("dp", "mp"), None),
            P(("dp", "mp"), None),
        ),
        out_specs=(P(None, "mp"), P("mp", None)),
        check_vma=False,
    )
```

```python
import functools
import math

import jax
import jax.numpy as jnp
from jax import lax
from jax.experimental import pallas as pl
from jax.experimental.pallas import tpu as pltpu
from jax.sharding import PartitionSpec as P

MESH = pl.DeviceIdType.MESH
HIGH = lax.Precision.HIGHEST
F32 = jnp.float32
BF16 = jnp.bfloat16
NX = 4
NC = 2


def dot(a, b, dims=((1,), (0,)), precision=None):
    return lax.dot_general(a, b, (dims, ((), ())), precision=precision, preferred_element_type=F32)


def split(v):
    hi = v.astype(BF16)
    return hi, (v - hi.astype(F32)).astype(BF16)


def remote(src, dst, ssem, rsem, where):
    return pltpu.make_async_remote_copy(
        src_ref=src, dst_ref=dst, send_sem=ssem, recv_sem=rsem, device_id=where, device_id_type=MESH
    )


def drain(view, sem):
    pltpu.make_async_copy(view, view, sem).wait()


def kernel(
    n_dp, n_mp, nodes, factor,
    x_hbm, w_in, w_out, src, weight, mask, rows_of, all_i, all_o,
    xv, hv, dv, ypv, ot, ot2, at, s16, cw, abuf, bsend, bbuf, ybf, sbuf, rbuf, tbuf, qbuf, aty, degs, own, hib, lob, clo, dcol,
    d_send, d_in, d_all, pc, gacc, oacc, gi, go,
    g_send, g_in, g_xy, g_all, w,
    ci_r, co_r, xi_s, xo_s, xi_r, xo_r, zi_s, zo_s, zi_r, zo_r, zo_a,
    ld_s, rs_s, rs_r, x_s, d_s, x_r, ar_s, ar_r, ag_s, ag_r, s_s, s_r, b_s, b_r,
):
    me = lax.axis_index("dp")
    my = lax.axis_index("mp")
    nz = n_dp // (NX * NC)
    ng = nz * NC
    zi, xi, ci = me // (NX * NC), me // NC % NX, me % NC
    gidx = zi * NC + ci
    pidx = xi * n_mp + my
    right, left, opp = (my + 1) % n_mp, (my + n_mp - 1) % n_mp, (my + 2) % n_mp
    rows, width = ybf.shape
    half = rows // 2
    recv = rbuf.shape[0]
    slots = recv // n_dp
    pairs = src.shape[0]

    def load(i, q):
        some = pl.ds(pl.multiple_of(q * rows, rows), rows)
        return pltpu.make_async_copy(x_hbm.at[some], xv.at[some], ld_s.at[i])

    loads = [load(i, q) for i, q in enumerate((opp, right, left, my))]
    for c in loads:
        c.start()

    barrier = pltpu.get_barrier_semaphore()

    @pl.loop(1, n_dp)
    def _(k):
        pl.semaphore_signal(barrier, inc=1, device_id=((me + k) % n_dp, my), device_id_type=MESH)

    @pl.loop(1, n_mp)
    def _(k):
        pl.semaphore_signal(barrier, inc=1, device_id=(me, (my + k) % n_mp), device_id_type=MESH)

    for dx in range(1, NX):
        for dy in range(1, n_mp):
            other = (zi * NX + (xi + dx) % NX) * NC + ci
            pl.semaphore_signal(barrier, inc=1, device_id=(other, (my + dy) % n_mp), device_id_type=MESH)

    def part_of(ref, q, part):
        return ref.at[pl.ds(pl.multiple_of(q * rows + part * half, half), half)]

    r_a = remote(bsend.at[4], abuf.at[0], rs_s.at[0], rs_r.at[0], (me, right))
    l_a = remote(bsend.at[5], abuf.at[1], rs_s.at[1], rs_r.at[1], (me, left))
    r_b = remote(bsend.at[0], bbuf.at[0, 1], rs_s.at[2], rs_r.at[2], (me, right))
    l_b = remote(bsend.at[1], bbuf.at[1, 0], rs_s.at[3], rs_r.at[3], (me, left))
    r_c = remote(bsend.at[2], bbuf.at[0, 0], rs_s.at[4], rs_r.at[4], (me, right))
    l_c = remote(bsend.at[3], bbuf.at[1, 1], rs_s.at[5], rs_r.at[5], (me, left))

    def pick(k, values):
        v = values[0]
        for i in range(1, len(values)):
            v = jnp.where(k == i, values[i], v)
        return v

    def forward(k, _):
        for i, at_step in enumerate((0, 2, 3, 6)):
            @pl.when(k == at_step)
            def _():
                loads[i].wait()

        q = pick(k, (opp, opp, right, left, right, left, my, my))
        part = pick(k, (0, 1, 1, 0, 0, 1, 0, 1))
        some = pl.ds(pl.multiple_of(q * rows + part * half, half), half)
        pre = dot(xv[some], w_in[...])
        sig = jax.nn.sigmoid(pre)
        hidden = (pre * sig).astype(BF16)
        hv[some] = hidden
        dv[some] = sig * (1.0 + pre * (1.0 - sig))
        ypv[some] = dot(hidden, w_out[...])

        @pl.when(k == 4)
        def _():
            def sel_body(g, _):
                base = pl.multiple_of(g * 32, 32)
                r = lax.broadcasted_iota(jnp.int32, (32, 128), 0) + base
                for lc in range(recv // 128):
                    lanes = slice(lc * 128, lc * 128 + 128)
                    one = jnp.broadcast_to(rows_of[0:1, lanes], (32, 128))
                    low = jnp.where(one == r, 1.0, 0.0).astype(BF16)
                    high = jnp.where(one == r + half, 1.0, 0.0).astype(BF16)
                    ot[pl.ds(base, 32), lanes] = low
                    ot[pl.ds(base + half, 32), lanes] = high
                    ot2[pl.ds(base, 32), lanes] = low + high
                return 0

            lax.fori_loop(0, half // 32, sel_body, 0)

        @pl.when(k == 1)
        def _():
            pl.semaphore_wait(barrier, n_dp - 1 + n_mp - 1 + (NX - 1) * (n_mp - 1))
            bsend[4] = part_of(ypv, opp, 0)[...].astype(BF16)
            bsend[5] = part_of(ypv, opp, 1)[...].astype(BF16)
            r_a.start()
            l_a.start()

        @pl.when(k == 2)
        def _():
            bsend[0] = part_of(ypv, right, 1)[...].astype(BF16)
            r_b.start()

        @pl.when(k == 3)
        def _():
            bsend[1] = part_of(ypv, left, 0)[...].astype(BF16)
            l_b.start()

        return 0

    lax.fori_loop(0, 8, forward, 0)

    s_all, c_all = src[...], weight[...] * mask[...].astype(F32)
    total = c_all
    for k in range(1, pairs):
        hit = pltpu.roll(s_all, k, 0) == s_all
        total = total + jnp.where(hit, pltpu.roll(c_all, k, 0), 0.0)
    cw[...] = total.astype(BF16)
    s16[...] = s_all.astype(jnp.int16)

    span = 64

    def pair_chunk(lc):
        lanes = slice(lc * 128, lc * 128 + 128)
        s_l, c_l = s16[:, lanes], cw[:, lanes]
        ss = [jnp.broadcast_to(s_l[p : p + 1], (span, 128)) for p in range(pairs)]
        cs = [jnp.broadcast_to(c_l[p : p + 1], (span, 128)) for p in range(pairs)]

        def body(g, _):
            base = pl.multiple_of(g * span, span)
            r = (lax.broadcasted_iota(jnp.int32, (span, 128), 0) + base).astype(jnp.int16)
            acc = jnp.zeros((span, 128), BF16)
            for p in range(pairs):
                acc = jnp.where(ss[p] == r, cs[p], acc)
            at[pl.ds(base, span), lanes] = acc
            return 0

        lax.fori_loop(0, recv // span, body, 0)

    chunks = rows // 128
    for lc in range(3 * chunks // 8):
        pair_chunk(lc)
    r_a.wait_recv()
    bsend[2] = (abuf[0].astype(F32) + part_of(ypv, right, 0)[...]).astype(BF16)
    r_c.start()
    l_a.wait_recv()
    bsend[3] = (abuf[1].astype(F32) + part_of(ypv, left, 1)[...]).astype(BF16)
    l_c.start()
    late = chunks - 3
    for lc in range(3 * chunks // 8, late):
        pair_chunk(lc)
    for c in (r_b, l_b, r_c, l_c):
        c.wait_recv()
    y = (
        ypv[pl.ds(pl.multiple_of(my * rows, rows), rows)]
        + bbuf[0].reshape(rows, width).astype(F32)
        + bbuf[1].reshape(rows, width).astype(F32)
    )
    ybf[...] = y.astype(BF16)
    y_b = ybf[...]
    y_t = jnp.transpose(y_b.astype(F32)).astype(BF16)
    gram = dot(y_t, y_b)

    def group_device(k):
        return (k // NC * NX + xi) * NC + k % NC

    def sum_start(which, value):
        g_send[which] = value.reshape(ng, 8, width)
        g_in[which, gidx] = g_send[which, gidx]

        @pl.loop(1, ng)
        def _(k):
            peer = (gidx + k) % ng
            remote(g_send.at[which, peer], g_in.at[which, gidx], ar_s.at[which, 0], ar_r.at[which, 0], (group_device(peer), my)).start()

    def plane_device(k):
        return (zi * NX + k // n_mp) * NC + ci, k % n_mp

    def sum_plane(which):
        drain(g_in.at[which, pl.ds(0, ng - 1)], ar_r.at[which, 0])
        t = g_in[which, 0]
        for k in range(1, ng):
            t = t + g_in[which, k]
        g_xy[which, pidx] = t

        @pl.loop(1, NX * n_mp)
        def _(k):
            remote(g_xy.at[which, pidx], g_xy.at[which, pidx], ar_s.at[which, 1], ar_r.at[which, 1], plane_device((pidx + k) % (NX * n_mp))).start()

    def sum_back(which):
        drain(g_xy.at[which, pl.ds(0, NX * n_mp - 1)], ar_r.at[which, 1])
        t = g_xy[which, 0]
        for k in range(1, NX * n_mp):
            t = t + g_xy[which, k]
        g_all[which, gidx] = t

        @pl.loop(1, ng)
        def _(k):
            peer = (gidx + k) % ng
            remote(g_all.at[which, gidx], g_all.at[which, gidx], ar_s.at[which, 2], ar_r.at[which, 2], (group_device(peer), my)).start()

    def sum_end(which):
        drain(g_all.at[which, pl.ds(0, ng - 1)], ar_r.at[which, 2])
        return g_all[which].reshape(width, width) * (1.0 / nodes)

    sum_start(0, gram)

    turns = [(nz // 2,)] + [(k, nz - k) for k in range(nz // 2 - 1, 0, -1)] + [(0,)]
    layer = NX * NC
    wide = layer * slots

    def layer_rows(k):
        return pl.ds(pl.multiple_of((zi + k) % nz * wide, wide), wide)

    def send_layer(source, target, i, k):
        zc = (zi + k) % nz
        for j in range(layer):
            peer = zc * layer + j

            def send():
                remote(
                    source.at[pl.ds(pl.multiple_of(peer * slots, slots), slots)],
                    target.at[pl.ds(pl.multiple_of(me * slots, slots), slots)],
                    x_s.at[i, k], x_r.at[i], (peer, my),
                ).start()

            if k:
                send()
            else:
                pl.when(peer != me)(send)

    def sent_layer(source, i, k):
        drain(source.at[pl.ds(0, wide if k else wide - slots)], x_s.at[i, k])

    mine = pl.ds(pl.multiple_of(me * slots, slots), slots)
    y_t2 = jnp.concatenate([y_t[:, :half], y_t[:, half:]], axis=0)
    y_ones = jnp.concatenate([y_b, jnp.ones((rows, width), BF16)], axis=1)

    def gather_layer(k):
        lanes = layer_rows(k)
        both = dot(y_t2, ot2[:, lanes])
        rows_k = jnp.where(jnp.broadcast_to(rows_of[0:1, lanes] < half, (width, wide)), both[:width], both[width:])
        sbuf[lanes] = jnp.transpose(rows_k).astype(BF16)

    def weigh_layer(k):
        some = pl.ds(k * wide, wide)
        both = dot(at[some], y_ones)
        aty[some] = both
        c_hi, c_lo = split(both[:, :width])
        tbuf[some] = c_hi
        clo[some] = c_lo
        for j in range(wide // 128):
            d_send[wide // 128 * k + j] = jnp.transpose(both[j * 128 : j * 128 + 128, width:])[0:1]

    plan = [(0, t) for t in turns] + [(1, t) for t in (turns[2], turns[3], turns[4], turns[0], turns[1])]
    first = len(turns)

    def send_turn(n):
        if n >= 2:
            i, layers = plan[n - 2]
            for k in layers:
                sent_layer((sbuf, tbuf)[i], i, k)
        i, layers = plan[n]
        for k in layers:
            send_layer((sbuf, tbuf)[i], (rbuf, qbuf)[i], i, k)

    weighed = 0
    for t, turn in enumerate(turns):
        for k in turn:
            gather_layer(k)
        send_turn(t)
        if late + t < chunks:
            pair_chunk(late + t)
        for _ in range(0 if t < 2 else 3 if t < 4 else 2):
            weigh_layer(weighed)
            weighed += 1
        if t == 2:
            sum_plane(0)
    rbuf[mine] = sbuf[mine]
    qbuf[mine] = tbuf[mine]
    sum_back(0)
    send_turn(first)
    send_turn(first + 1)
    ones_r = jnp.ones((width, recv), BF16)

    def deg_body(k, _):
        lanes = pl.ds(pl.multiple_of(k * 256, 256), 256)
        degs[lanes] = jnp.transpose(dot(ones_r, at[:, lanes]))
        return 0

    lax.fori_loop(0, rows // 256, deg_body, 0)

    o_hi, o_lo = split(degs[...] * y_b.astype(F32))
    s_own = dot(y_t, o_hi) + dot(y_t, o_lo)

    drain(rbuf.at[pl.ds(0, recv - slots)], x_r.at[0])
    r_t = jnp.transpose(rbuf[...].astype(F32)).astype(BF16)

    def back_body(k, _):
        some = pl.ds(pl.multiple_of(k * wide, wide), wide)
        both = aty[some]
        b_hi, b_lo = split(both[:, width:] * rbuf[some].astype(F32) - both[:, :width])
        hib[some] = b_hi
        lob[some] = b_lo
        return 0

    lax.fori_loop(0, nz, back_body, 0)

    mixed = dot(r_t, tbuf[...]) + dot(r_t, clo[...])
    s_part = s_own + (dot(r_t, hib[...]) + dot(r_t, lob[...])) - jnp.transpose(mixed)
    sum_start(1, s_part)
    send_turn(first + 2)


    per = 128 // slots

    @pl.loop(1, n_dp)
    def _(k):
        peer = (me + k) % n_dp
        remote(d_send.at[peer // per], d_in.at[me], d_s, x_r.at[2], (peer, my)).start()

    d_in[me] = d_send[me // per]
    gram_n = sum_end(0)
    w[...] = gram_n
    lane = lax.broadcasted_iota(jnp.int32, (width, width), 1)
    sub = lax.broadcasted_iota(jnp.int32, (width, width), 0)

    def sweep(i, _):
        k = pl.multiple_of(2 * i, 2)
        a = w[...]
        r0, r1 = w[pl.ds(k, 1), :], w[pl.ds(k + 1, 1), :]
        m0, m1 = lane == k, lane == k + 1
        c0 = jnp.sum(jnp.where(m0, a, 0.0), axis=1, keepdims=True)
        c1 = jnp.sum(jnp.where(m1, a, 0.0), axis=1, keepdims=True)
        p = jnp.sum(jnp.where(m0[0:1], r0, 0.0), axis=1, keepdims=True)
        q = jnp.sum(jnp.where(m1[0:1], r0, 0.0), axis=1, keepdims=True)
        d = jnp.sum(jnp.where(m1[0:1], r1, 0.0), axis=1, keepdims=True)
        ip = 1.0 / p
        f = q * ip
        e11 = 1.0 / (d - q * f)
        e01 = -f * e11
        e00 = ip - f * e01
        t0, t1 = e00 * r0 + e01 * r1, e01 * r0 + e11 * r1
        new = a - (c0 * t0 + c1 * t1)
        new = jnp.where(m0, e00 * c0 + e01 * c1, jnp.where(m1, e01 * c0 + e11 * c1, new))
        w[...] = new
        w[pl.ds(k, 1), :] = jnp.where(m0[0:1], -e00, jnp.where(m1[0:1], -e01, t0))
        w[pl.ds(k + 1, 1), :] = jnp.where(m0[0:1], -e01, jnp.where(m1[0:1], -e11, t1))
        return 0

    steps = width // 2

    def own_body(k, _):
        lanes = pl.ds(pl.multiple_of(k * 256, 256), 256)
        cross = jnp.transpose(dot(r_t, at[:, lanes]))
        own[lanes] = degs[lanes] * ybf[lanes].astype(F32) - cross
        return 0

    lax.fori_loop(0, rows // 256, own_body, 0)
    fifth = steps // 5

    def sweeps(t):
        lax.fori_loop(t * fifth, steps if t == 4 else (t + 1) * fifth, sweep, 0)

    sweeps(0)
    send_turn(first + 3)
    sweeps(1)
    sum_plane(1)
    send_turn(first + 4)
    sweeps(2)
    sweeps(3)
    sum_back(1)
    sweeps(4)
    drain(d_in.at[pl.ds(0, n_dp - 1)], x_r.at[2])
    d_all[...] = pltpu.roll(d_in[...].reshape(n_dp, 128), (128 - slots * (me % per)) % 128, 1)
    spot = lax.broadcasted_iota(jnp.int32, (recv // 128, 128), 1) // slots
    d_row = jnp.zeros((recv // 128, 128), F32)
    for j in range(per):
        piece = d_all[pl.ds(j, recv // 128, stride=per), :]
        d_row = jnp.where(spot == j, pltpu.roll(piece, slots * j, 1), d_row)
    for k in range(recv // 128):
        column = jnp.transpose(jnp.broadcast_to(d_row[k : k + 1], (128, width)))
        d_hi, d_lo = split(column)
        dcol[k * 128 : k * 128 + 128] = jnp.where(lane < width // 2, d_hi.astype(F32), d_lo.astype(F32)).astype(BF16)

    def add_body(k, _):
        some = pl.ds(pl.multiple_of(k * 256, 256), 256)
        extra = dot(ot[some], dcol[...])
        own[some] = own[some] + (extra[:, 0:1] + extra[:, width - 1 :]) * ybf[some].astype(F32)
        return 0

    lax.fori_loop(0, rows // 256, add_body, 0)
    inv0 = -w[...]
    eye2 = jnp.where(lane == sub, 2.0, 0.0)
    inverse = dot(inv0, eye2 - dot(gram_n, inv0, precision=HIGH), precision=HIGH)
    i_hi, i_lo = split(inverse * factor)
    i_both = jnp.concatenate([i_hi, i_lo], axis=1)
    s_n = sum_end(1)
    b0 = dot(inverse, s_n, precision=HIGH)
    b1 = b0 + dot(inverse, s_n - dot(gram_n, b0, precision=HIGH), precision=HIGH)
    b_hi = b1.astype(BF16)
    rest = b1 - b_hi.astype(F32)
    b_mid = rest.astype(BF16)
    b_lo = (rest - b_mid.astype(F32)).astype(BF16)
    b_low = jnp.concatenate([b_mid, b_lo], axis=1)

    def remove_body(k, _):
        some = pl.ds(pl.multiple_of(k * 256, 256), 256)
        yk = ybf[some]
        low = dot(yk, b_low)
        own[some] = own[some] - (dot(yk, b_hi) + (low[:, :width] + low[:, width:]))
        return 0

    lax.fori_loop(0, rows // 256, remove_body, 0)
    drain(qbuf.at[pl.ds(0, recv - slots)], x_r.at[1])

    gathers = []
    for i, (q, part, to) in enumerate(
        ((my, 0, right), (my, 1, left), (my, 1, right), (my, 0, left), (left, 0, right), (right, 1, left))
    ):
        gathers.append(remote(part_of(pc, q, part), part_of(pc, q, part), ag_s.at[i], ag_r.at[i], (me, to)))

    def grad_body(k, _):
        some = pl.ds(pl.multiple_of(k * 256, 256), 256)
        n_hi, n_lo = split(own[some] - dot(ot[some], qbuf[...]))
        both = dot(n_hi, i_both)
        gy = both[:, :width] + (both[:, width:] + dot(n_lo, i_hi))
        pc[pl.ds(pl.multiple_of(my * rows + k * 256, 256), 256)] = gy.astype(BF16)

        @pl.when(k == half // 256 - 1)
        def _():
            gathers[0].start()

        return 0

    lax.fori_loop(0, rows // 256, grad_body, 0)
    for c in gathers[1:4]:
        c.start()
    gacc[...] = jnp.zeros_like(gacc)
    oacc[...] = jnp.zeros_like(oacc)

    def backward(k, _):
        for i, (at_step, then) in enumerate(((2, 4), (3, 5), (4, None), (5, None), (6, None), (7, None))):
            @pl.when(k == at_step)
            def _():
                gathers[i].wait_recv()
                if then is not None:
                    gathers[then].start()

        q = pick(k, (my, my, left, right, left, right, opp, opp))
        part = pick(k, (0, 1, 0, 1, 1, 0, 0, 1))
        some = pl.ds(pl.multiple_of(q * rows + part * half, half), half)
        gy = pc[some]
        dh = dot(gy, w_out[...], ((1,), (1,)))
        gp_t = jnp.transpose(dh * dv[some]).astype(BF16)
        gacc[...] += dot(gp_t, xv[some])
        oacc[...] += dot(jnp.transpose(gy.astype(F32)).astype(BF16), hv[some])
        return 0

    lax.fori_loop(0, 8, backward, 0)
    gi[...] = jnp.transpose(gacc[...])
    go[...] = jnp.transpose(oacc[...])

    x, z, c = xi, zi, ci

    def at_x(k):
        return ((z * NX + k) * NC + c, my)

    def at_z(k):
        return ((k * NX + x) * NC + c, my)

    mate = (me - c + (1 - c), my)
    hi, ho = xi_s.shape[0], xo_s.shape[0]
    qi, qo = hi // NX, ho // NX
    ti = qi // nz
    theirs_i = pl.ds(pl.multiple_of((1 - c) * hi, hi), hi)
    theirs_o = pl.ds(pl.multiple_of((1 - c) * ho, ho), ho)
    mine_i = pl.ds(pl.multiple_of(c * hi, hi), hi)
    mine_o = pl.ds(pl.multiple_of(c * ho, ho), ho)
    c_i = remote(gi.at[theirs_i], ci_r, s_s.at[0], s_r.at[0], mate)
    c_o = remote(go.at[theirs_o], co_r, s_s.at[1], s_r.at[1], mate)
    c_i.start()
    c_o.start()
    c_i.wait_recv()
    c_o.wait_recv()
    ci_r[...] = gi[mine_i] + ci_r[...]
    co_r[...] = go[mine_o] + co_r[...]
    xi_s[...] = ci_r[...].astype(BF16)
    xo_s[...] = co_r[...].astype(BF16)
    sent = [c_i, c_o]
    xs = []
    for k in (2, 1, 3):
        p = (x + k) % NX
        a = remote(xi_s.at[pl.ds(pl.multiple_of(p * qi, qi), qi)], xi_r.at[k - 1], s_s.at[2 * k], s_r.at[2 * k], at_x(p))
        b = remote(xo_s.at[pl.ds(pl.multiple_of(p * qo, qo), qo)], xo_r.at[k - 1], s_s.at[2 * k + 1], s_r.at[2 * k + 1], at_x(p))
        a.start()
        b.start()
        xs += [a, b]
    for d in xs:
        d.wait_recv()
    sent += xs
    t_i = ci_r[pl.ds(pl.multiple_of(x * qi, qi), qi)]
    t_o = co_r[pl.ds(pl.multiple_of(x * qo, qo), qo)]
    for k in range(NX - 1):
        t_i = t_i + xi_r[k].astype(F32)
        t_o = t_o + xo_r[k].astype(F32)
    zi_s[...] = t_i.astype(BF16)
    zo_s[...] = t_o.reshape(zo_s.shape)
    zo_r[z] = zo_s[z]
    zi_r[z] = zi_s[pl.ds(pl.multiple_of(z * ti, ti), ti)]
    order = sorted(range(1, nz), key=lambda k: -min(k, nz - k))
    for k in order:
        p = (z + k) % nz
        remote(zi_s.at[pl.ds(pl.multiple_of(p * ti, ti), ti)], zi_r.at[z], b_s.at[0], b_r.at[0], at_z(p)).start()
        remote(zo_s.at[p], zo_r.at[z], b_s.at[1], b_r.at[1], at_z(p)).start()

    drain(zi_r.at[pl.ds(0, nz - 1)], b_r.at[0])
    f_i = zi_r[0].astype(F32)
    for k in range(1, nz):
        f_i = f_i + zi_r[k].astype(F32)
    block_i = pl.ds(pl.multiple_of(c * hi + x * qi + z * ti, ti), ti)
    all_i[block_i] = f_i.astype(BF16)
    for k in order:
        remote(all_i.at[block_i], all_i.at[block_i], b_s.at[2], b_r.at[2], at_z((z + k) % nz)).start()
    drain(zo_r.at[pl.ds(0, nz - 1)], b_r.at[1])
    f_o = zo_r[0]
    for k in range(1, nz):
        f_o = f_o + zo_r[k]
    zo_a[z] = f_o
    for k in order:
        remote(zo_a.at[z], zo_a.at[z], b_s.at[7], b_r.at[7], at_z((z + k) % nz)).start()
    drain(zi_s.at[pl.ds(0, (nz - 1) * ti)], b_r.at[2])
    drain(zo_a.at[pl.ds(0, nz - 1)], b_r.at[7])
    quarter_o = pl.ds(pl.multiple_of(c * ho + x * qo, qo), qo)
    all_o[quarter_o] = zo_a[...].reshape(qo, width).astype(BF16)
    quarter_i = pl.ds(pl.multiple_of(c * hi + x * qi, qi), qi)
    for k in (2, 1, 3):
        remote(all_i.at[quarter_i], all_i.at[quarter_i], b_s.at[4], b_r.at[4], at_x((x + k) % NX)).start()
        remote(all_o.at[quarter_o], all_o.at[quarter_o], b_s.at[3], b_r.at[3], at_x((x + k) % NX)).start()
    drain(xo_s.at[pl.ds(0, (NX - 1) * qo)], b_r.at[3])
    d_o = remote(all_o.at[mine_o], all_o.at[mine_o], b_s.at[5], b_r.at[5], mate)
    d_o.start()
    drain(xi_s.at[pl.ds(0, (NX - 1) * qi)], b_r.at[4])
    d_i = remote(all_i.at[mine_i], all_i.at[mine_i], b_s.at[6], b_r.at[6], mate)
    d_i.start()
    for which in range(2):
        drain(g_send.at[which, pl.ds(0, ng - 1)], ar_s.at[which, 0])
        drain(g_xy.at[which, pl.ds(0, NX * n_mp - 1)], ar_s.at[which, 1])
        drain(g_all.at[which, pl.ds(0, ng - 1)], ar_s.at[which, 2])
    for d in gathers + [r_a, l_a, r_b, l_b, r_c, l_c]:
        d.wait_send()
    for i, layers in plan[-2:]:
        for k in layers:
            sent_layer(tbuf, i, k)
    drain(d_in.at[pl.ds(0, n_dp - 1)], d_s)
    drain(zi_r.at[pl.ds(0, nz - 1)], b_s.at[0])
    drain(zo_r.at[pl.ds(0, nz - 1)], b_s.at[1])
    drain(zi_s.at[pl.ds(0, (nz - 1) * ti)], b_s.at[2])
    drain(zo_a.at[pl.ds(0, nz - 1)], b_s.at[7])
    drain(xo_s.at[pl.ds(0, (NX - 1) * qo)], b_s.at[3])
    drain(xi_s.at[pl.ds(0, (NX - 1) * qi)], b_s.at[4])
    for d in sent + [d_o, d_i]:
        d.wait_send()
    d_o.wait_recv()
    d_i.wait_recv()


def whole(features, w_in, w_out, src_t, weight_t, mask_t, send_row, n_dp, n_mp, nodes, factor):
    group, depth = features.shape
    units, width = w_out.shape
    rows = group // n_mp
    recv = send_row.shape[1]
    pairs = src_t.shape[0]
    nz = n_dp // (NX * NC)
    ng = n_dp // NX
    hi, ho = depth // NC, units // NC
    qi, qo = hi // NX, ho // NX
    vm = pltpu.VMEM
    dma = pltpu.SemaphoreType.DMA
    return pl.pallas_call(
        functools.partial(kernel, n_dp, n_mp, nodes, factor),
        out_shape=(jax.ShapeDtypeStruct((depth, units), BF16), jax.ShapeDtypeStruct((units, width), BF16)),
        in_specs=[pl.BlockSpec(memory_space=pl.ANY)] + [pl.BlockSpec(memory_space=vm)] * 6,
        out_specs=[pl.BlockSpec(memory_space=vm)] * 2,
        scratch_shapes=[
            vm((group, depth), BF16), vm((group, units), BF16), vm((group, units), F32), vm((group, width), F32),
            vm((rows, recv), BF16), vm((rows // 2, recv), BF16), vm((recv, rows), BF16), vm((pairs, rows), jnp.int16), vm((pairs, rows), BF16),
            vm((2, rows // 2, width), BF16), vm((6, rows // 2, width), BF16), vm((2, 2, rows // 2, width), BF16),
            vm((rows, width), BF16),
            vm((recv, width), BF16), vm((recv, width), BF16), vm((recv, width), BF16), vm((recv, width), BF16),
            vm((recv, 2 * width), F32), vm((rows, width), F32), vm((rows, width), F32),
            vm((recv, width), BF16), vm((recv, width), BF16), vm((recv, width), BF16), vm((recv, width), BF16),
            vm((recv // 128, 1, 128), F32), vm((n_dp, 1, 128), F32), vm((n_dp, 128), F32),
            vm((group, width), BF16), vm((units, depth), F32), vm((width, units), F32),
            vm((depth, units), F32), vm((units, width), F32),
            vm((2, ng, 8, width), F32), vm((2, ng, 8, width), F32), vm((2, NX * n_mp, 8, width), F32),
            vm((2, ng, 8, width), F32), vm((width, width), F32),
            vm((hi, units), F32), vm((ho, width), F32), vm((hi, units), BF16), vm((ho, width), BF16),
            vm((NX - 1, qi, units), BF16), vm((NX - 1, qo, width), BF16),
            vm((qi, units), BF16), vm((nz, qo // nz, width), F32), vm((nz, qi // nz, units), BF16), vm((nz, qo // nz, width), F32),
            vm((nz, qo // nz, width), F32),
            dma((4,)), dma((6,)), dma((6,)), dma((2, nz)), dma, dma((3,)), dma((2, 3)), dma((2, 3)), dma((6,)), dma((6,)),
            dma((8,)), dma((8,)), dma((8,)), dma((8,)),
        ],
        compiler_params=pltpu.CompilerParams(collective_id=0, has_side_effects=True, vmem_limit_bytes=58 << 20),
        name="step",
    )(features, w_in, w_out, src_t, weight_t, mask_t, send_row)


def widen_kernel(a, b, oa, ob):
    oa[...] = a[...].astype(F32)
    ob[...] = b[...].astype(F32)


def widen(a, b):
    vm = pl.BlockSpec(memory_space=pltpu.VMEM)
    return pl.pallas_call(
        widen_kernel,
        out_shape=(jax.ShapeDtypeStruct(a.shape, F32), jax.ShapeDtypeStruct(b.shape, F32)),
        in_specs=[vm] * 2,
        out_specs=[vm] * 2,
        name="widen",
    )(a, b)


def shards(features, w_in, w_out, send_rows, pair_src, pair_weight, pair_mask):
    n_dp = lax.axis_size("dp")
    n_mp = lax.axis_size("mp")
    nodes = features.shape[0] * n_dp
    pairs = pair_src.shape[1]
    scale = 1.0 / (pairs * math.sqrt(nodes))
    return widen(
        *whole(
            features, w_in, w_out, pair_src.T, pair_weight.T, pair_mask.T, send_rows.reshape(1, -1),
            n_dp, n_mp, nodes, 2.0 * scale,
        )
    )


def solution(mesh):
    return jax.shard_map(
        shards,
        mesh=mesh,
        in_specs=(
            P("dp", None),
            P(None, "mp"),
            P("mp", None),
            P(("dp", "mp")),
            P(("dp", "mp"), None),
            P(("dp", "mp"), None),
            P(("dp", "mp"), None),
        ),
        out_specs=(P(None, "mp"), P("mp", None)),
        check_vma=False,
    )
```

```python
import functools
import math

import jax
import jax.numpy as jnp
from jax import lax
from jax.experimental import pallas as pl
from jax.experimental.pallas import tpu as pltpu
from jax.sharding import PartitionSpec as P

MESH = pl.DeviceIdType.MESH
HIGH = lax.Precision.HIGHEST
F32 = jnp.float32
BF16 = jnp.bfloat16
NX = 4
NC = 2


def dot(a, b, dims=((1,), (0,)), precision=None):
    return lax.dot_general(a, b, (dims, ((), ())), precision=precision, preferred_element_type=F32)


def split(v):
    hi = v.astype(BF16)
    return hi, (v - hi.astype(F32)).astype(BF16)


def remote(src, dst, ssem, rsem, where):
    return pltpu.make_async_remote_copy(
        src_ref=src, dst_ref=dst, send_sem=ssem, recv_sem=rsem, device_id=where, device_id_type=MESH
    )


def drain(view, sem):
    pltpu.make_async_copy(view, view, sem).wait()


def kernel(
    n_dp, n_mp, nodes, factor,
    x_hbm, w_in, w_out, src, weight, mask, rows_of, all_i, all_o,
    xv, hv, dv, ypv, ot, ot2, at, s16, cw, abuf, bsend, bbuf, ybf, sbuf, rbuf, tbuf, qbuf, aty, degs, own, hib, lob, clo, dcol,
    d_send, d_in, d_all, pc, gacc, oacc, gi, go,
    g_send, g_in, g_xy, g_all, w,
    ci_r, co_r, xi_s, xo_s, xi_r, xo_r, zi_s, zo_s, zi_r, zo_r, zo_a,
    ld_s, rs_s, rs_r, x_s, d_s, x_r, ar_s, ar_r, ag_s, ag_r, s_s, s_r, b_s, b_r,
):
    me = lax.axis_index("dp")
    my = lax.axis_index("mp")
    nz = n_dp // (NX * NC)
    ng = nz * NC
    zi, xi, ci = me // (NX * NC), me // NC % NX, me % NC
    gidx = zi * NC + ci
    pidx = xi * n_mp + my
    right, left, opp = (my + 1) % n_mp, (my + n_mp - 1) % n_mp, (my + 2) % n_mp
    rows, width = ybf.shape
    half = rows // 2
    recv = rbuf.shape[0]
    slots = recv // n_dp
    pairs = src.shape[0]

    def load(i, q):
        some = pl.ds(pl.multiple_of(q * rows, rows), rows)
        return pltpu.make_async_copy(x_hbm.at[some], xv.at[some], ld_s.at[i])

    loads = [load(i, q) for i, q in enumerate((opp, right, left, my))]
    for c in loads:
        c.start()

    barrier = pltpu.get_barrier_semaphore()

    @pl.loop(1, n_dp)
    def _(k):
        pl.semaphore_signal(barrier, inc=1, device_id=((me + k) % n_dp, my), device_id_type=MESH)

    @pl.loop(1, n_mp)
    def _(k):
        pl.semaphore_signal(barrier, inc=1, device_id=(me, (my + k) % n_mp), device_id_type=MESH)

    for dx in range(1, NX):
        for dy in range(1, n_mp):
            other = (zi * NX + (xi + dx) % NX) * NC + ci
            pl.semaphore_signal(barrier, inc=1, device_id=(other, (my + dy) % n_mp), device_id_type=MESH)

    def part_of(ref, q, part):
        return ref.at[pl.ds(pl.multiple_of(q * rows + part * half, half), half)]

    r_a = remote(bsend.at[4], abuf.at[0], rs_s.at[0], rs_r.at[0], (me, right))
    l_a = remote(bsend.at[5], abuf.at[1], rs_s.at[1], rs_r.at[1], (me, left))
    r_b = remote(bsend.at[0], bbuf.at[0, 1], rs_s.at[2], rs_r.at[2], (me, right))
    l_b = remote(bsend.at[1], bbuf.at[1, 0], rs_s.at[3], rs_r.at[3], (me, left))
    r_c = remote(bsend.at[2], bbuf.at[0, 0], rs_s.at[4], rs_r.at[4], (me, right))
    l_c = remote(bsend.at[3], bbuf.at[1, 1], rs_s.at[5], rs_r.at[5], (me, left))

    def pick(k, values):
        v = values[0]
        for i in range(1, len(values)):
            v = jnp.where(k == i, values[i], v)
        return v

    def forward(k, _):
        for i, at_step in enumerate((0, 2, 3, 6)):
            @pl.when(k == at_step)
            def _():
                loads[i].wait()

        q = pick(k, (opp, opp, right, left, right, left, my, my))
        part = pick(k, (0, 1, 1, 0, 0, 1, 0, 1))
        some = pl.ds(pl.multiple_of(q * rows + part * half, half), half)
        pre = dot(xv[some], w_in[...])
        sig = jax.nn.sigmoid(pre)
        hidden = (pre * sig).astype(BF16)
        hv[some] = hidden
        dv[some] = sig * (1.0 + pre * (1.0 - sig))
        ypv[some] = dot(hidden, w_out[...])

        @pl.when(k == 4)
        def _():
            def sel_body(g, _):
                base = pl.multiple_of(g * 32, 32)
                r = lax.broadcasted_iota(jnp.int32, (32, 128), 0) + base
                for lc in range(recv // 128):
                    lanes = slice(lc * 128, lc * 128 + 128)
                    one = jnp.broadcast_to(rows_of[0:1, lanes], (32, 128))
                    low = jnp.where(one == r, 1.0, 0.0).astype(BF16)
                    high = jnp.where(one == r + half, 1.0, 0.0).astype(BF16)
                    ot[pl.ds(base, 32), lanes] = low
                    ot[pl.ds(base + half, 32), lanes] = high
                    ot2[pl.ds(base, 32), lanes] = low + high
                return 0

            lax.fori_loop(0, half // 32, sel_body, 0)

        @pl.when(k == 1)
        def _():
            pl.semaphore_wait(barrier, n_dp - 1 + n_mp - 1 + (NX - 1) * (n_mp - 1))
            bsend[4] = part_of(ypv, opp, 0)[...].astype(BF16)
            bsend[5] = part_of(ypv, opp, 1)[...].astype(BF16)
            r_a.start()
            l_a.start()

        @pl.when(k == 2)
        def _():
            bsend[0] = part_of(ypv, right, 1)[...].astype(BF16)
            r_b.start()

        @pl.when(k == 3)
        def _():
            bsend[1] = part_of(ypv, left, 0)[...].astype(BF16)
            l_b.start()

        return 0

    lax.fori_loop(0, 8, forward, 0)

    s_all, c_all = src[...], weight[...] * mask[...].astype(F32)
    total = c_all
    for k in range(1, pairs):
        hit = pltpu.roll(s_all, k, 0) == s_all
        total = total + jnp.where(hit, pltpu.roll(c_all, k, 0), 0.0)
    cw[...] = total.astype(BF16)
    s16[...] = s_all.astype(jnp.int16)

    span = 64

    def pair_chunk(lc):
        lanes = slice(lc * 128, lc * 128 + 128)
        s_l, c_l = s16[:, lanes], cw[:, lanes]
        ss = [jnp.broadcast_to(s_l[p : p + 1], (span, 128)) for p in range(pairs)]
        cs = [jnp.broadcast_to(c_l[p : p + 1], (span, 128)) for p in range(pairs)]

        def body(g, _):
            base = pl.multiple_of(g * span, span)
            r = (lax.broadcasted_iota(jnp.int32, (span, 128), 0) + base).astype(jnp.int16)
            acc = jnp.zeros((span, 128), BF16)
            for p in range(pairs):
                acc = jnp.where(ss[p] == r, cs[p], acc)
            at[pl.ds(base, span), lanes] = acc
            return 0

        lax.fori_loop(0, recv // span, body, 0)

    chunks = rows // 128
    for lc in range(3 * chunks // 8):
        pair_chunk(lc)
    r_a.wait_recv()
    bsend[2] = (abuf[0].astype(F32) + part_of(ypv, right, 0)[...]).astype(BF16)
    r_c.start()
    l_a.wait_recv()
    bsend[3] = (abuf[1].astype(F32) + part_of(ypv, left, 1)[...]).astype(BF16)
    l_c.start()
    late = chunks - 3
    for lc in range(3 * chunks // 8, late):
        pair_chunk(lc)
    for c in (r_b, l_b, r_c, l_c):
        c.wait_recv()
    y = (
        ypv[pl.ds(pl.multiple_of(my * rows, rows), rows)]
        + bbuf[0].reshape(rows, width).astype(F32)
        + bbuf[1].reshape(rows, width).astype(F32)
    )
    ybf[...] = y.astype(BF16)
    y_b = ybf[...]
    y_t = jnp.transpose(y_b.astype(F32)).astype(BF16)
    gram = dot(y_t, y_b)

    def group_device(k):
        return (k // NC * NX + xi) * NC + k % NC

    def sum_start(which, value):
        g_send[which] = value.reshape(ng, 8, width)
        g_in[which, gidx] = g_send[which, gidx]

        @pl.loop(1, ng)
        def _(k):
            peer = (gidx + k) % ng
            remote(g_send.at[which, peer], g_in.at[which, gidx], ar_s.at[which, 0], ar_r.at[which, 0], (group_device(peer), my)).start()

    def plane_device(k):
        return (zi * NX + k // n_mp) * NC + ci, k % n_mp

    def sum_plane(which):
        drain(g_in.at[which, pl.ds(0, ng - 1)], ar_r.at[which, 0])
        t = g_in[which, 0]
        for k in range(1, ng):
            t = t + g_in[which, k]
        g_xy[which, pidx] = t

        @pl.loop(1, NX * n_mp)
        def _(k):
            remote(g_xy.at[which, pidx], g_xy.at[which, pidx], ar_s.at[which, 1], ar_r.at[which, 1], plane_device((pidx + k) % (NX * n_mp))).start()

    def sum_back(which):
        drain(g_xy.at[which, pl.ds(0, NX * n_mp - 1)], ar_r.at[which, 1])
        t = g_xy[which, 0]
        for k in range(1, NX * n_mp):
            t = t + g_xy[which, k]
        g_all[which, gidx] = t

        @pl.loop(1, ng)
        def _(k):
            peer = (gidx + k) % ng
            remote(g_all.at[which, gidx], g_all.at[which, gidx], ar_s.at[which, 2], ar_r.at[which, 2], (group_device(peer), my)).start()

    def sum_end(which):
        drain(g_all.at[which, pl.ds(0, ng - 1)], ar_r.at[which, 2])
        return g_all[which].reshape(width, width) * (1.0 / nodes)

    sum_start(0, gram)

    turns = [(nz // 2,)] + [(k, nz - k) for k in range(nz // 2 - 1, 0, -1)] + [(0,)]
    layer = NX * NC
    wide = layer * slots

    def layer_rows(k):
        return pl.ds(pl.multiple_of((zi + k) % nz * wide, wide), wide)

    def send_layer(source, target, i, k):
        zc = (zi + k) % nz
        for j in range(layer):
            peer = zc * layer + j

            def send():
                remote(
                    source.at[pl.ds(pl.multiple_of(peer * slots, slots), slots)],
                    target.at[pl.ds(pl.multiple_of(me * slots, slots), slots)],
                    x_s.at[i, k], x_r.at[i], (peer, my),
                ).start()

            if k:
                send()
            else:
                pl.when(peer != me)(send)

    def sent_layer(source, i, k):
        drain(source.at[pl.ds(0, wide if k else wide - slots)], x_s.at[i, k])

    mine = pl.ds(pl.multiple_of(me * slots, slots), slots)
    y_t2 = jnp.concatenate([y_t[:, :half], y_t[:, half:]], axis=0)
    y_ones = jnp.concatenate([y_b, jnp.ones((rows, width), BF16)], axis=1)

    def gather_layer(k):
        lanes = layer_rows(k)
        both = dot(y_t2, ot2[:, lanes])
        rows_k = jnp.where(jnp.broadcast_to(rows_of[0:1, lanes] < half, (width, wide)), both[:width], both[width:])
        sbuf[lanes] = jnp.transpose(rows_k).astype(BF16)

    def weigh_layer(k):
        some = pl.ds(k * wide, wide)
        both = dot(at[some], y_ones)
        aty[some] = both
        c_hi, c_lo = split(both[:, :width])
        tbuf[some] = c_hi
        clo[some] = c_lo
        for j in range(wide // 128):
            d_send[wide // 128 * k + j] = jnp.transpose(both[j * 128 : j * 128 + 128, width:])[0:1]

    plan = [(0, t) for t in turns] + [(1, t) for t in (turns[2], turns[3], turns[4], turns[0], turns[1])]
    first = len(turns)

    def send_turn(n):
        if n >= 2:
            i, layers = plan[n - 2]
            for k in layers:
                sent_layer((sbuf, tbuf)[i], i, k)
        i, layers = plan[n]
        for k in layers:
            send_layer((sbuf, tbuf)[i], (rbuf, qbuf)[i], i, k)

    weighed = 0
    for t, turn in enumerate(turns):
        for k in turn:
            gather_layer(k)
        send_turn(t)
        if late + t < chunks:
            pair_chunk(late + t)
        for _ in range(0 if t < 2 else 3 if t < 4 else 2):
            weigh_layer(weighed)
            weighed += 1
        if t == 2:
            sum_plane(0)
    rbuf[mine] = sbuf[mine]
    qbuf[mine] = tbuf[mine]
    sum_back(0)
    send_turn(first)
    send_turn(first + 1)
    ones_r = jnp.ones((width, recv), BF16)

    def deg_body(k, _):
        lanes = pl.ds(pl.multiple_of(k * 256, 256), 256)
        degs[lanes] = jnp.transpose(dot(ones_r, at[:, lanes]))
        return 0

    lax.fori_loop(0, rows // 256, deg_body, 0)

    o_hi, o_lo = split(degs[...] * y_b.astype(F32))
    s_own = dot(y_t, o_hi) + dot(y_t, o_lo)

    drain(rbuf.at[pl.ds(0, recv - slots)], x_r.at[0])
    r_t = jnp.transpose(rbuf[...].astype(F32)).astype(BF16)

    def back_body(k, _):
        some = pl.ds(pl.multiple_of(k * wide, wide), wide)
        both = aty[some]
        b_hi, b_lo = split(both[:, width:] * rbuf[some].astype(F32) - both[:, :width])
        hib[some] = b_hi
        lob[some] = b_lo
        return 0

    lax.fori_loop(0, nz, back_body, 0)

    mixed = dot(r_t, tbuf[...]) + dot(r_t, clo[...])
    s_part = s_own + (dot(r_t, hib[...]) + dot(r_t, lob[...])) - jnp.transpose(mixed)
    sum_start(1, s_part)
    send_turn(first + 2)


    per = 128 // slots

    @pl.loop(1, n_dp)
    def _(k):
        peer = (me + k) % n_dp
        remote(d_send.at[peer // per], d_in.at[me], d_s, x_r.at[2], (peer, my)).start()

    d_in[me] = d_send[me // per]
    gram_n = sum_end(0)
    w[...] = gram_n
    lane = lax.broadcasted_iota(jnp.int32, (width, width), 1)
    sub = lax.broadcasted_iota(jnp.int32, (width, width), 0)

    def sweep(i, _):
        k = pl.multiple_of(2 * i, 2)
        a = w[...]
        r0, r1 = w[pl.ds(k, 1), :], w[pl.ds(k + 1, 1), :]
        m0, m1 = lane == k, lane == k + 1
        c0 = jnp.sum(jnp.where(m0, a, 0.0), axis=1, keepdims=True)
        c1 = jnp.sum(jnp.where(m1, a, 0.0), axis=1, keepdims=True)
        p = jnp.sum(jnp.where(m0[0:1], r0, 0.0), axis=1, keepdims=True)
        q = jnp.sum(jnp.where(m1[0:1], r0, 0.0), axis=1, keepdims=True)
        d = jnp.sum(jnp.where(m1[0:1], r1, 0.0), axis=1, keepdims=True)
        ip = 1.0 / p
        f = q * ip
        e11 = 1.0 / (d - q * f)
        e01 = -f * e11
        e00 = ip - f * e01
        t0, t1 = e00 * r0 + e01 * r1, e01 * r0 + e11 * r1
        new = a - (c0 * t0 + c1 * t1)
        new = jnp.where(m0, e00 * c0 + e01 * c1, jnp.where(m1, e01 * c0 + e11 * c1, new))
        w[...] = new
        w[pl.ds(k, 1), :] = jnp.where(m0[0:1], -e00, jnp.where(m1[0:1], -e01, t0))
        w[pl.ds(k + 1, 1), :] = jnp.where(m0[0:1], -e01, jnp.where(m1[0:1], -e11, t1))
        return 0

    steps = width // 2

    def own_body(k, _):
        lanes = pl.ds(pl.multiple_of(k * 256, 256), 256)
        cross = jnp.transpose(dot(r_t, at[:, lanes]))
        own[lanes] = degs[lanes] * ybf[lanes].astype(F32) - cross
        return 0

    lax.fori_loop(0, rows // 256, own_body, 0)
    fifth = steps // 5

    def sweeps(t):
        lax.fori_loop(t * fifth, steps if t == 4 else (t + 1) * fifth, sweep, 0)

    sweeps(0)
    send_turn(first + 3)
    sweeps(1)
    sum_plane(1)
    send_turn(first + 4)
    sweeps(2)
    sweeps(3)
    sum_back(1)
    sweeps(4)
    drain(d_in.at[pl.ds(0, n_dp - 1)], x_r.at[2])
    d_all[...] = pltpu.roll(d_in[...].reshape(n_dp, 128), (128 - slots * (me % per)) % 128, 1)
    spot = lax.broadcasted_iota(jnp.int32, (recv // 128, 128), 1) // slots
    d_row = jnp.zeros((recv // 128, 128), F32)
    for j in range(per):
        piece = d_all[pl.ds(j, recv // 128, stride=per), :]
        d_row = jnp.where(spot == j, pltpu.roll(piece, slots * j, 1), d_row)
    for k in range(recv // 128):
        column = jnp.transpose(jnp.broadcast_to(d_row[k : k + 1], (128, width)))
        d_hi, d_lo = split(column)
        dcol[k * 128 : k * 128 + 128] = jnp.where(lane < width // 2, d_hi.astype(F32), d_lo.astype(F32)).astype(BF16)

    def add_body(k, _):
        some = pl.ds(pl.multiple_of(k * 256, 256), 256)
        extra = dot(ot[some], dcol[...])
        own[some] = own[some] + (extra[:, 0:1] + extra[:, width - 1 :]) * ybf[some].astype(F32)
        return 0

    lax.fori_loop(0, rows // 256, add_body, 0)
    inv0 = -w[...]
    eye2 = jnp.where(lane == sub, 2.0, 0.0)
    inverse = dot(inv0, eye2 - dot(gram_n, inv0, precision=HIGH), precision=HIGH)
    i_hi, i_lo = split(inverse * factor)
    i_both = jnp.concatenate([i_hi, i_lo], axis=1)
    s_n = sum_end(1)
    b0 = dot(inverse, s_n, precision=HIGH)
    b1 = b0 + dot(inverse, s_n - dot(gram_n, b0, precision=HIGH), precision=HIGH)
    b_hi = b1.astype(BF16)
    rest = b1 - b_hi.astype(F32)
    b_mid = rest.astype(BF16)
    b_lo = (rest - b_mid.astype(F32)).astype(BF16)
    b_low = jnp.concatenate([b_mid, b_lo], axis=1)

    def remove_body(k, _):
        some = pl.ds(pl.multiple_of(k * 256, 256), 256)
        yk = ybf[some]
        low = dot(yk, b_low)
        own[some] = own[some] - (dot(yk, b_hi) + (low[:, :width] + low[:, width:]))
        return 0

    lax.fori_loop(0, rows // 256, remove_body, 0)
    drain(qbuf.at[pl.ds(0, recv - slots)], x_r.at[1])

    gathers = []
    for i, (q, part, to) in enumerate(
        ((my, 0, right), (my, 1, left), (my, 1, right), (my, 0, left), (left, 0, right), (right, 1, left))
    ):
        gathers.append(remote(part_of(pc, q, part), part_of(pc, q, part), ag_s.at[i], ag_r.at[i], (me, to)))

    def grad_body(k, _):
        some = pl.ds(pl.multiple_of(k * 256, 256), 256)
        n_hi, n_lo = split(own[some] - dot(ot[some], qbuf[...]))
        both = dot(n_hi, i_both)
        gy = both[:, :width] + (both[:, width:] + dot(n_lo, i_hi))
        pc[pl.ds(pl.multiple_of(my * rows + k * 256, 256), 256)] = gy.astype(BF16)

        @pl.when(k == half // 256 - 1)
        def _():
            gathers[0].start()
            gathers[3].start()

        return 0

    lax.fori_loop(0, rows // 256, grad_body, 0)
    for c in gathers[1:3]:
        c.start()
    gacc[...] = jnp.zeros_like(gacc)
    oacc[...] = jnp.zeros_like(oacc)

    def backward(k, _):
        for i, (at_step, then) in enumerate(((2, 4), (3, 5), (4, None), (5, None), (6, None), (7, None))):
            @pl.when(k == at_step)
            def _():
                gathers[i].wait_recv()
                if then is not None:
                    gathers[then].start()

        q = pick(k, (my, my, left, right, left, right, opp, opp))
        part = pick(k, (0, 1, 0, 1, 1, 0, 0, 1))
        some = pl.ds(pl.multiple_of(q * rows + part * half, half), half)
        gy = pc[some]
        dh = dot(gy, w_out[...], ((1,), (1,)))
        gp_t = jnp.transpose(dh * dv[some]).astype(BF16)
        gacc[...] += dot(gp_t, xv[some])
        oacc[...] += dot(jnp.transpose(gy.astype(F32)).astype(BF16), hv[some])
        return 0

    lax.fori_loop(0, 8, backward, 0)
    gi[...] = jnp.transpose(gacc[...])
    go[...] = jnp.transpose(oacc[...])

    x, z, c = xi, zi, ci

    def at_x(k):
        return ((z * NX + k) * NC + c, my)

    def at_z(k):
        return ((k * NX + x) * NC + c, my)

    mate = (me - c + (1 - c), my)
    hi, ho = xi_s.shape[0], xo_s.shape[0]
    qi, qo = hi // NX, ho // NX
    ti = qi // nz
    theirs_i = pl.ds(pl.multiple_of((1 - c) * hi, hi), hi)
    theirs_o = pl.ds(pl.multiple_of((1 - c) * ho, ho), ho)
    mine_i = pl.ds(pl.multiple_of(c * hi, hi), hi)
    mine_o = pl.ds(pl.multiple_of(c * ho, ho), ho)
    c_i = remote(gi.at[theirs_i], ci_r, s_s.at[0], s_r.at[0], mate)
    c_o = remote(go.at[theirs_o], co_r, s_s.at[1], s_r.at[1], mate)
    c_i.start()
    c_o.start()
    c_i.wait_recv()
    c_o.wait_recv()
    ci_r[...] = gi[mine_i] + ci_r[...]
    co_r[...] = go[mine_o] + co_r[...]
    xi_s[...] = ci_r[...].astype(BF16)
    xo_s[...] = co_r[...].astype(BF16)
    sent = [c_i, c_o]
    xs = []
    for k in (2, 1, 3):
        p = (x + k) % NX
        a = remote(xi_s.at[pl.ds(pl.multiple_of(p * qi, qi), qi)], xi_r.at[k - 1], s_s.at[2 * k], s_r.at[2 * k], at_x(p))
        b = remote(xo_s.at[pl.ds(pl.multiple_of(p * qo, qo), qo)], xo_r.at[k - 1], s_s.at[2 * k + 1], s_r.at[2 * k + 1], at_x(p))
        a.start()
        b.start()
        xs += [a, b]
    for d in xs:
        d.wait_recv()
    sent += xs
    t_i = ci_r[pl.ds(pl.multiple_of(x * qi, qi), qi)]
    t_o = co_r[pl.ds(pl.multiple_of(x * qo, qo), qo)]
    for k in range(NX - 1):
        t_i = t_i + xi_r[k].astype(F32)
        t_o = t_o + xo_r[k].astype(F32)
    zi_s[...] = t_i.astype(BF16)
    zo_s[...] = t_o.reshape(zo_s.shape)
    zo_r[z] = zo_s[z]
    zi_r[z] = zi_s[pl.ds(pl.multiple_of(z * ti, ti), ti)]
    order = sorted(range(1, nz), key=lambda k: -min(k, nz - k))
    for k in order:
        p = (z + k) % nz
        remote(zi_s.at[pl.ds(pl.multiple_of(p * ti, ti), ti)], zi_r.at[z], b_s.at[0], b_r.at[0], at_z(p)).start()
        remote(zo_s.at[p], zo_r.at[z], b_s.at[1], b_r.at[1], at_z(p)).start()

    drain(zi_r.at[pl.ds(0, nz - 1)], b_r.at[0])
    f_i = zi_r[0].astype(F32)
    for k in range(1, nz):
        f_i = f_i + zi_r[k].astype(F32)
    block_i = pl.ds(pl.multiple_of(c * hi + x * qi + z * ti, ti), ti)
    all_i[block_i] = f_i.astype(BF16)
    for k in order:
        remote(all_i.at[block_i], all_i.at[block_i], b_s.at[2], b_r.at[2], at_z((z + k) % nz)).start()
    drain(zo_r.at[pl.ds(0, nz - 1)], b_r.at[1])
    f_o = zo_r[0]
    for k in range(1, nz):
        f_o = f_o + zo_r[k]
    zo_a[z] = f_o
    for k in order:
        remote(zo_a.at[z], zo_a.at[z], b_s.at[7], b_r.at[7], at_z((z + k) % nz)).start()
    drain(zi_s.at[pl.ds(0, (nz - 1) * ti)], b_r.at[2])
    drain(zo_a.at[pl.ds(0, nz - 1)], b_r.at[7])
    quarter_o = pl.ds(pl.multiple_of(c * ho + x * qo, qo), qo)
    all_o[quarter_o] = zo_a[...].reshape(qo, width).astype(BF16)
    quarter_i = pl.ds(pl.multiple_of(c * hi + x * qi, qi), qi)
    for k in (2, 1, 3):
        remote(all_i.at[quarter_i], all_i.at[quarter_i], b_s.at[4], b_r.at[4], at_x((x + k) % NX)).start()
        remote(all_o.at[quarter_o], all_o.at[quarter_o], b_s.at[3], b_r.at[3], at_x((x + k) % NX)).start()
    drain(xo_s.at[pl.ds(0, (NX - 1) * qo)], b_r.at[3])
    d_o = remote(all_o.at[mine_o], all_o.at[mine_o], b_s.at[5], b_r.at[5], mate)
    d_o.start()
    drain(xi_s.at[pl.ds(0, (NX - 1) * qi)], b_r.at[4])
    d_i = remote(all_i.at[mine_i], all_i.at[mine_i], b_s.at[6], b_r.at[6], mate)
    d_i.start()
    for which in range(2):
        drain(g_send.at[which, pl.ds(0, ng - 1)], ar_s.at[which, 0])
        drain(g_xy.at[which, pl.ds(0, NX * n_mp - 1)], ar_s.at[which, 1])
        drain(g_all.at[which, pl.ds(0, ng - 1)], ar_s.at[which, 2])
    for d in gathers + [r_a, l_a, r_b, l_b, r_c, l_c]:
        d.wait_send()
    for i, layers in plan[-2:]:
        for k in layers:
            sent_layer(tbuf, i, k)
    drain(d_in.at[pl.ds(0, n_dp - 1)], d_s)
    drain(zi_r.at[pl.ds(0, nz - 1)], b_s.at[0])
    drain(zo_r.at[pl.ds(0, nz - 1)], b_s.at[1])
    drain(zi_s.at[pl.ds(0, (nz - 1) * ti)], b_s.at[2])
    drain(zo_a.at[pl.ds(0, nz - 1)], b_s.at[7])
    drain(xo_s.at[pl.ds(0, (NX - 1) * qo)], b_s.at[3])
    drain(xi_s.at[pl.ds(0, (NX - 1) * qi)], b_s.at[4])
    for d in sent + [d_o, d_i]:
        d.wait_send()
    d_o.wait_recv()
    d_i.wait_recv()


def whole(features, w_in, w_out, src_t, weight_t, mask_t, send_row, n_dp, n_mp, nodes, factor):
    group, depth = features.shape
    units, width = w_out.shape
    rows = group // n_mp
    recv = send_row.shape[1]
    pairs = src_t.shape[0]
    nz = n_dp // (NX * NC)
    ng = n_dp // NX
    hi, ho = depth // NC, units // NC
    qi, qo = hi // NX, ho // NX
    vm = pltpu.VMEM
    dma = pltpu.SemaphoreType.DMA
    return pl.pallas_call(
        functools.partial(kernel, n_dp, n_mp, nodes, factor),
        out_shape=(jax.ShapeDtypeStruct((depth, units), BF16), jax.ShapeDtypeStruct((units, width), BF16)),
        in_specs=[pl.BlockSpec(memory_space=pl.ANY)] + [pl.BlockSpec(memory_space=vm)] * 6,
        out_specs=[pl.BlockSpec(memory_space=vm)] * 2,
        scratch_shapes=[
            vm((group, depth), BF16), vm((group, units), BF16), vm((group, units), F32), vm((group, width), F32),
            vm((rows, recv), BF16), vm((rows // 2, recv), BF16), vm((recv, rows), BF16), vm((pairs, rows), jnp.int16), vm((pairs, rows), BF16),
            vm((2, rows // 2, width), BF16), vm((6, rows // 2, width), BF16), vm((2, 2, rows // 2, width), BF16),
            vm((rows, width), BF16),
            vm((recv, width), BF16), vm((recv, width), BF16), vm((recv, width), BF16), vm((recv, width), BF16),
            vm((recv, 2 * width), F32), vm((rows, width), F32), vm((rows, width), F32),
            vm((recv, width), BF16), vm((recv, width), BF16), vm((recv, width), BF16), vm((recv, width), BF16),
            vm((recv // 128, 1, 128), F32), vm((n_dp, 1, 128), F32), vm((n_dp, 128), F32),
            vm((group, width), BF16), vm((units, depth), F32), vm((width, units), F32),
            vm((depth, units), F32), vm((units, width), F32),
            vm((2, ng, 8, width), F32), vm((2, ng, 8, width), F32), vm((2, NX * n_mp, 8, width), F32),
            vm((2, ng, 8, width), F32), vm((width, width), F32),
            vm((hi, units), F32), vm((ho, width), F32), vm((hi, units), BF16), vm((ho, width), BF16),
            vm((NX - 1, qi, units), BF16), vm((NX - 1, qo, width), BF16),
            vm((qi, units), BF16), vm((nz, qo // nz, width), F32), vm((nz, qi // nz, units), BF16), vm((nz, qo // nz, width), F32),
            vm((nz, qo // nz, width), F32),
            dma((4,)), dma((6,)), dma((6,)), dma((2, nz)), dma, dma((3,)), dma((2, 3)), dma((2, 3)), dma((6,)), dma((6,)),
            dma((8,)), dma((8,)), dma((8,)), dma((8,)),
        ],
        compiler_params=pltpu.CompilerParams(collective_id=0, has_side_effects=True, vmem_limit_bytes=58 << 20),
        name="step",
    )(features, w_in, w_out, src_t, weight_t, mask_t, send_row)


def widen_kernel(a, b, oa, ob):
    oa[...] = a[...].astype(F32)
    ob[...] = b[...].astype(F32)


def widen(a, b):
    vm = pl.BlockSpec(memory_space=pltpu.VMEM)
    return pl.pallas_call(
        widen_kernel,
        out_shape=(jax.ShapeDtypeStruct(a.shape, F32), jax.ShapeDtypeStruct(b.shape, F32)),
        in_specs=[vm] * 2,
        out_specs=[vm] * 2,
        name="widen",
    )(a, b)


def shards(features, w_in, w_out, send_rows, pair_src, pair_weight, pair_mask):
    n_dp = lax.axis_size("dp")
    n_mp = lax.axis_size("mp")
    nodes = features.shape[0] * n_dp
    pairs = pair_src.shape[1]
    scale = 1.0 / (pairs * math.sqrt(nodes))
    return widen(
        *whole(
            features, w_in, w_out, pair_src.T, pair_weight.T, pair_mask.T, send_rows.reshape(1, -1),
            n_dp, n_mp, nodes, 2.0 * scale,
        )
    )


def solution(mesh):
    return jax.shard_map(
        shards,
        mesh=mesh,
        in_specs=(
            P("dp", None),
            P(None, "mp"),
            P("mp", None),
            P(("dp", "mp")),
            P(("dp", "mp"), None),
            P(("dp", "mp"), None),
            P(("dp", "mp"), None),
        ),
        out_specs=(P(None, "mp"), P("mp", None)),
        check_vma=False,
    )
```
